256 devices in a mesh: clique: 8 (over y_hi, x), copy: 32 (over z, y_lo, core).
Axes of the slice: x: 4, y: 4 (y_hi: 2, y_lo: 2; y = y_hi * 2 + y_lo), z: 8, core: 2. Of those that a mesh axis runs over, the one named last changes fastest.
Arguments:
- out_grad: bfloat16 [524288, 512], P(('clique', 'copy')), may hold values from -6 to 6
- pre_act: bfloat16 [524288, 512], P(('clique', 'copy')), may hold values from -6 to 6
- batch_count: int32 [256], P(('clique', 'copy')), may hold values from 1024 to 2048, as said below
- layer_two: bfloat16 [512, 512], replicated, may hold values from -0.25 to 0.25
- hot_slots: int32 [524288, 10], P(('clique', 'copy')), may hold values from 0 to 4095
- cold_index: int32 [524288, 15], P(('clique', 'copy')), may hold values from 0 to 2047
- hot_feats: bfloat16 [4096, 768], P('clique'), may hold values from -6 to 6
- cold_feats: bfloat16 [524288, 768], P(('clique', 'copy')), may hold values from -6 to 6
Outputs:
- grad_one: float32 [768, 512], replicated
- grad_two: float32 [512, 512], replicated
The draws below stay inside these ranges and needn't reach their ends.
Inputs may be any that keep to these rules, and one draw needn't show every extreme that they name: `batch_count`: some device has all 2048 rows live in every draw.
All inputs are finite; a program needn't handle non-finite values.
Results may differ from the reference program's by a relative error of at most 0.015.
Values may be sent and summed in bfloat16 or wider, within the bound.
A program may use at most 128 MiB of HBM per device.

```python
import math
import jax
import jax.numpy as jnp
import numpy as np
from jax import lax

D_IN = 768
D_H = 512
B_DEV = 2048
C_DEV = 2048
K_HOT = 10
K_COLD = 15
FANOUT = 25
HOT = 4096
DEVS = 256
TARGETS = 524288
COLD = 524288
N_CLIQUE = 8
N_COPY = 32


def draw_batch_count(key, part):
    counts = jax.random.randint(jax.random.fold_in(key, 11), (DEVS,), B_DEV // 2, B_DEV + 1)
    full_at = jax.random.randint(jax.random.fold_in(key, 12), (), 0, DEVS)
    return counts.at[full_at].set(B_DEV).astype(jnp.int32)


def touch_ends(array, stream_key, low, high):
    extent = array.shape
    place = [jax.random.randint(jax.random.fold_in(stream_key, axis), (), 0, extent[axis]) for axis in range(len(extent))]
    array = array.at[tuple(place)].set(low)
    longest = extent.index(max(extent))
    place[longest] = (place[longest] + 1) % extent[longest]
    return array.at[tuple(place)].set(high)


def block_scale(own_key, shape, cuts, smallest, largest):
    def one(axis_at, parts):
        steps = jax.random.uniform(jax.random.fold_in(jax.random.fold_in(own_key, 6), axis_at), (parts,), jnp.float32, smallest / len(cuts), largest / len(cuts))
        return jnp.repeat(jnp.exp(steps), shape[axis_at] // parts).reshape((-1,) + (1,) * (len(shape) - axis_at - 1))

    loudness = one(*cuts[0])
    for cut in cuts[1:]:
        loudness = loudness * one(*cut)
    return loudness


def rank_bounds(count, lean):
    loads = [(1 << 20) // math.isqrt(standing ** lean) + 1 for standing in range(1, count + 1)]
    spread = 1 + sum(loads) // (1 << 30)
    return np.cumsum(np.array([max(1, weight // spread) for weight in loads]))


def ranked_ids(rng, shape, number_of, skew):
    listing = rank_bounds(number_of, skew)
    ticket = jax.random.randint(jax.random.fold_in(rng, 1), shape, 0, int(listing[number_of - 1]))
    standing = jnp.searchsorted(jnp.asarray(listing, jnp.int32), ticket, side="right")
    return jax.random.permutation(jax.random.fold_in(rng, 2), number_of)[standing].astype(jnp.int32)


def bell_draw(key, shape, width, bound, split=(), held_as=jnp.bfloat16):
    array = width * jax.random.normal(key, shape, jnp.float32)
    if split:
        array = array * block_scale(key, shape, split, -0.22, 0.18)
    return jnp.clip(array, -bound, bound).astype(held_as)


def setup_inputs(seed: int = 0) -> dict:
    splits = jax.random.split(jax.random.key(seed), 9)
    out_grad = bell_draw(splits[0], (TARGETS, D_H), 1.0, 6.0, ((0, 256),))
    pre_act = bell_draw(splits[1], (TARGETS, D_H), 1.0, 6.0, ((0, 256),))
    batch_count = draw_batch_count(jax.random.fold_in(splits[8], 71), 0)
    layer_two = bell_draw(splits[3], (D_H, D_H), D_H ** -0.5, 0.25)
    hot_slots = touch_ends(ranked_ids(splits[4], (TARGETS, K_HOT), HOT, 2), jax.random.fold_in(splits[4], 3), 0, HOT - 1).astype(jnp.int32)
    cold_index = touch_ends(jax.random.randint(splits[5], (TARGETS, K_COLD), 0, C_DEV), jax.random.fold_in(splits[5], 1), 0, C_DEV - 1).astype(jnp.int32)
    hot_feats = bell_draw(splits[6], (HOT, D_IN), 1.0, 6.0, ((0, 8),))
    cold_feats = bell_draw(splits[7], (COLD, D_IN), 1.0, 6.0, ((0, 256),))
    return dict(out_grad=out_grad, pre_act=pre_act, batch_count=batch_count, layer_two=layer_two, hot_slots=hot_slots, cold_index=cold_index, hot_feats=hot_feats, cold_feats=cold_feats)


def device_terms(out_grad, pre_act, count, layer_two, hot_slots, cold_index, cold_feats):
    live = (jnp.arange(B_DEV, dtype=jnp.int32) < count)[:, None]
    masked = jnp.where(live, out_grad, jnp.zeros_like(out_grad))
    activ = jnp.maximum(pre_act, jnp.zeros_like(pre_act))
    grad_two = jnp.dot(activ.T, masked, preferred_element_type=jnp.float32)
    back = jnp.dot(masked, layer_two.T, preferred_element_type=jnp.float32)
    row_grad = jnp.where(pre_act > 0, back, jnp.zeros_like(back)).astype(jnp.bfloat16)
    rows_wide = row_grad.astype(jnp.float32)
    hot_part = jnp.zeros((HOT, D_H), jnp.float32)
    for column in range(K_HOT):
        hot_part = hot_part.at[hot_slots[:, column]].add(rows_wide)
    hot_part = (hot_part * (1.0 / FANOUT)).astype(jnp.bfloat16)
    cold_part = jnp.zeros((C_DEV, D_H), jnp.float32)
    for column in range(K_COLD):
        cold_part = cold_part.at[cold_index[:, column]].add(rows_wide)
    cold_part = (cold_part * (1.0 / FANOUT)).astype(jnp.bfloat16)
    grad_cold = jnp.dot(cold_feats.T, cold_part, preferred_element_type=jnp.float32)
    return hot_part, grad_cold, grad_two


def reference(out_grad, pre_act, batch_count, layer_two, hot_slots, cold_index, hot_feats, cold_feats):
    n_clq = N_CLIQUE
    n_cpy = N_COPY
    og = out_grad.reshape(n_clq, n_cpy, B_DEV, D_H)
    pa = pre_act.reshape(n_clq, n_cpy, B_DEV, D_H)
    bc = batch_count.reshape(n_clq, n_cpy)
    hs = hot_slots.reshape(n_clq, n_cpy, B_DEV, K_HOT)
    ci = cold_index.reshape(n_clq, n_cpy, B_DEV, K_COLD)
    cf = cold_feats.reshape(n_clq, n_cpy, C_DEV, D_IN)

    def per_copy(carry, j):
        grad_one, grad_two = carry

        def per_member(i, inner):
            hot_sum, g_one, g_two = inner
            hot_part, grad_cold, part_two = device_terms(og[i, j], pa[i, j], bc[i, j], layer_two, hs[i, j], ci[i, j], cf[i, j])
            return (hot_sum + hot_part.astype(jnp.float32), g_one + grad_cold, g_two + part_two)

        start = (jnp.zeros((HOT, D_H), jnp.float32), grad_one, grad_two)
        hot_sum, grad_one, grad_two = lax.fori_loop(0, n_clq, per_member, start)
        hot_b = hot_sum.astype(jnp.bfloat16)
        grad_one = grad_one + jnp.dot(hot_feats.T, hot_b, preferred_element_type=jnp.float32)
        return (grad_one, grad_two), None

    init = (jnp.zeros((D_IN, D_H), jnp.float32), jnp.zeros((D_H, D_H), jnp.float32))
    (grad_one, grad_two), _ = lax.scan(per_copy, init, jnp.arange(n_cpy, dtype=jnp.int32))
    return grad_one, grad_two
```

```python
import functools
import jax
import jax.numpy as jnp
from jax import lax
from jax.experimental import pallas as pl
from jax.experimental.pallas import tpu as pltpu
from jax.sharding import PartitionSpec as P

MESH = pl.DeviceIdType.MESH
BLK = 512
WB = BLK // 8
LANES = 128


def build_counts(idx_ref, block, c_ref):
    k_n, rows = idx_ref.shape
    sub = lax.broadcasted_iota(jnp.int32, (8, LANES), 0)
    for j in range(rows // LANES):
        cols = slice(j * LANES, j * LANES + LANES)
        local = idx_ref[:, cols] - block * BLK
        inside = (local >= 0) & (local < BLK)
        word = jnp.where(inside, local & (WB - 1), -1)
        unit = jnp.left_shift(jnp.ones_like(local), ((local >> 6) & 7) * 4)
        ws = [jnp.broadcast_to(word[k : k + 1], (8, LANES)) for k in range(k_n)]
        us = [jnp.broadcast_to(unit[k : k + 1], (8, LANES)) for k in range(k_n)]
        for pair in range(WB // 16):
            two = []
            for h in range(2):
                at = sub + (pair * 16 + h * 8)
                acc = jnp.where(ws[0] == at, us[0], 0)
                for k in range(1, k_n):
                    acc = acc + jnp.where(ws[k] == at, us[k], 0)
                two.append(acc)
            words = jnp.concatenate(two, 0)
            for b in range(8):
                field = (words >> (4 * b)) & 15
                at = b * WB + pair * 16
                c_ref[at : at + 16, cols] = field.astype(jnp.float32).astype(jnp.bfloat16)


def parts_kernel(
    fanout, cnt_ref, og_hbm, pa_hbm, l2_hbm, hs_hbm, ci_hbm, hp, two_ref, og, pa, l2, hs, ci, rg, c0, c1, sems
):
    rows = og.shape[0]
    tile = 512
    pairs = [(l2_hbm, l2), (og_hbm, og), (pa_hbm, pa), (ci_hbm, ci), (hs_hbm, hs)]
    copies = [pltpu.make_async_copy(s, d, sems.at[i]) for i, (s, d) in enumerate(pairs)]
    for c in copies:
        c.start()
    for c in copies:
        c.wait()
    count = cnt_ref[0]
    two_ref[...] = jnp.zeros_like(two_ref)

    def some_rows(i, carry):
        at = pl.ds(pl.multiple_of(i * tile, tile), tile)
        live = (lax.broadcasted_iota(jnp.int32, (tile, 1), 0) + i * tile) < count
        o = og[at, :]
        masked = jnp.where(live, o, jnp.zeros_like(o))
        p = pa[at, :]
        back = lax.dot_general(
            masked, l2[...], (((1,), (1,)), ((), ())), preferred_element_type=jnp.float32
        )
        rg[at, :] = jnp.where(p > 0, back, 0.0).astype(jnp.bfloat16)
        activ = jnp.maximum(p, jnp.zeros_like(p))
        two_ref[...] += lax.dot_general(
            activ, masked, (((0,), (0,)), ((), ())), preferred_element_type=jnp.float32
        )
        return carry

    lax.fori_loop(0, rows // tile, some_rows, 0)
    n_cold = 4
    n_hot = hp.shape[0] // BLK - n_cold

    def step(idx_ref, block, c_new, c_old, base):
        if idx_ref is not None:
            build_counts(idx_ref, block, c_new)
        p = jnp.dot(c_old[...], rg[...], preferred_element_type=jnp.float32)
        at = pl.ds(pl.multiple_of(base, BLK), BLK)
        hp[at, :] = (p * (1.0 / fanout)).astype(jnp.bfloat16)

    cold = n_hot * BLK
    build_counts(ci, 0, c0)
    step(ci, 1, c1, c0, cold)
    step(ci, 2, c0, c1, cold + BLK)
    step(ci, 3, c1, c0, cold + 2 * BLK)
    step(hs, 0, c0, c1, cold + 3 * BLK)

    def hot(i, carry):
        step(hs, 2 * i + 1, c1, c0, 2 * i * BLK)
        step(hs, 2 * i + 2, c0, c1, (2 * i + 1) * BLK)
        return carry

    lax.fori_loop(0, n_hot // 2 - 1, hot, 0)
    step(hs, n_hot - 1, c1, c0, (n_hot - 2) * BLK)
    step(None, 0, c0, c1, (n_hot - 1) * BLK)


def parts_call(fanout, og, pa, cnt, l2, hs, ci, slots):
    vm = pltpu.VMEM
    rows, dh = og.shape
    return pl.pallas_call(
        functools.partial(parts_kernel, fanout),
        out_shape=(
            jax.ShapeDtypeStruct((slots, dh), jnp.bfloat16),
            jax.ShapeDtypeStruct((dh, dh), jnp.float32),
        ),
        in_specs=[pl.BlockSpec(memory_space=pltpu.SMEM)] + [pl.BlockSpec(memory_space=pl.ANY)] * 5,
        out_specs=[pl.BlockSpec(memory_space=vm)] * 2,
        scratch_shapes=[
            vm((rows, dh), jnp.bfloat16),
            vm((rows, dh), jnp.bfloat16),
            vm((dh, dh), jnp.bfloat16),
            vm((hs.shape[1], rows), jnp.int32),
            vm((ci.shape[1], rows), jnp.int32),
            vm((rows, dh), jnp.bfloat16),
            vm((BLK, rows), jnp.bfloat16),
            vm((BLK, rows), jnp.bfloat16),
            pltpu.SemaphoreType.DMA((5,)),
        ],
        compiler_params=pltpu.CompilerParams(vmem_limit_bytes=48 << 20),
        cost_estimate=pl.CostEstimate(flops=15 * 10**9, bytes_accessed=10**7, transcendentals=0),
    )(cnt, og, pa, l2, hs.T, ci.T)


class Place:
    def __init__(self):
        clique, copy = lax.axis_index("clique"), lax.axis_index("copy")
        self.x, self.y = clique % 4, (clique // 4) * 2 + (copy // 2) % 2
        self.z, self.core = copy // 4, copy % 2
        self.member = self.x * 4 + self.y

    def device(self, x, y, z, core):
        return ((y // 2) * 4 + x, z * 4 + (y % 2) * 2 + core)

    def mate(self):
        return self.device(self.x, self.y, self.z, 1 - self.core)

    def plane(self):
        for dx in range(4):
            for dy in range(4):
                if dx or dy:
                    x, y = (self.x + dx) % 4, (self.y + dy) % 4
                    yield x * 4 + y, self.device(x, y, self.z, self.core)

    def column(self, steps):
        for dz in steps:
            z = (self.z + dz) % 8
            yield z, self.device(self.x, self.y, z, self.core)


def remote(src, dst, send, recv, device):
    return pltpu.make_async_remote_copy(
        src_ref=src, dst_ref=dst, send_sem=send, recv_sem=recv, device_id=device, device_id_type=MESH
    )


def sum_kernel(g_hbm, out_hbm, g, rc, hs, ra, ms, rb, out, sem, c_s, c_r, a_s, a_r, b_s, b_r, d_s, d_r, e_s, e_r, f_s, f_r):
    here = Place()
    half = rc.shape[0]
    per = half // 16
    load = pltpu.make_async_copy(g_hbm, g, sem.at[0])
    load.start()
    barrier = pltpu.get_barrier_semaphore()
    peers = [here.mate()] + [d for _, d in here.plane()] + [d for _, d in here.column(range(1, 8))]
    for d in peers:
        pl.semaphore_signal(barrier, inc=1, device_id=d, device_id_type=MESH)
    pl.semaphore_wait(barrier, len(peers))
    load.wait()
    mine, other = here.core * half, (1 - here.core) * half
    swap = remote(g.at[pl.ds(other, half)], rc, c_s, c_r, here.mate())
    swap.start()
    swap.wait()
    f32 = jnp.float32
    hs[...] = (g[pl.ds(mine, half)].astype(f32) + rc[...].astype(f32)).astype(jnp.bfloat16)
    sent = []
    for q, d in here.plane():
        c = remote(hs.at[pl.ds(q * per, per)], ra.at[here.member], a_s.at[q], a_r.at[here.member], d)
        c.start()
        sent.append(c)
    ra[here.member] = hs[pl.ds(here.member * per, per)]
    for q, d in here.plane():
        remote(hs.at[pl.ds(q * per, per)], ra.at[q], a_s.at[q], a_r.at[q], d).wait_recv()
    ms[...] = jnp.sum(ra[...].astype(f32), axis=0).astype(jnp.bfloat16)
    for z, d in here.column(range(1, 8)):
        at = pl.ds(pl.multiple_of((z % 4) * LANES, LANES), LANES)
        c = remote(ms.at[:, :, at], rb.at[here.z], b_s.at[z], b_r.at[here.z], d)
        c.start()
        sent.append(c)
    part = pl.ds(pl.multiple_of((here.z % 4) * LANES, LANES), LANES)
    rb[here.z] = ms[:, :, part]
    for z, d in here.column(range(1, 8)):
        remote(ms.at[:, :, part], rb.at[z], b_s.at[z], b_r.at[z], d).wait_recv()
    slot = pl.ds(mine + here.member * per, per)
    out[slot, :, part] = jnp.sum(rb[...].astype(f32), axis=0).astype(jnp.bfloat16)
    steps = (1, 7, 6)
    for n, (z, d) in enumerate(here.column(steps)):
        c = remote(out.at[slot, :, part], out.at[slot, :, part], d_s.at[n], d_r.at[n], d)
        c.start()
        sent.append(c)
    for n, (z, d) in enumerate(here.column([8 - s for s in steps])):
        theirs = pl.ds(pl.multiple_of((z % 4) * LANES, LANES), LANES)
        remote(out.at[slot, :, theirs], out.at[slot, :, theirs], d_s.at[n], d_r.at[n], d).wait_recv()
    for q, d in here.plane():
        c = remote(out.at[slot], out.at[slot], e_s.at[q], e_r.at[here.member], d)
        c.start()
        sent.append(c)
    c = remote(out.at[slot], out.at[slot], f_s.at[here.member], f_r.at[here.member], here.mate())
    c.start()
    sent.append(c)
    for q, d in here.plane():
        at = pl.ds(mine + q * per, per)
        remote(out.at[at], out.at[at], e_s.at[q], e_r.at[q], d).wait_recv()
        c = remote(out.at[at], out.at[at], f_s.at[q], f_r.at[q], here.mate())
        c.start()
        sent.append(c)
    for q in range(16):
        at = pl.ds(other + q * per, per)
        remote(out.at[at], out.at[at], f_s.at[q], f_r.at[q], here.mate()).wait_recv()
    for c in sent:
        c.wait_send()
    store = pltpu.make_async_copy(out, out_hbm, sem.at[1])
    store.start()
    store.wait()


def sum_call(g):
    vm, dma = pltpu.VMEM, pltpu.SemaphoreType.DMA
    units, _, dh = g.shape
    half, per, bf16 = units // 2, units // 32, jnp.bfloat16
    return pl.pallas_call(
        sum_kernel,
        out_shape=jax.ShapeDtypeStruct(g.shape, bf16),
        in_specs=[pl.BlockSpec(memory_space=pl.ANY)],
        out_specs=pl.BlockSpec(memory_space=pl.ANY),
        scratch_shapes=[
            vm(g.shape, bf16),
            vm((half, 8, dh), bf16),
            vm((half, 8, dh), bf16),
            vm((16, per, 8, dh), bf16),
            vm((per, 8, dh), bf16),
            vm((8, per, 8, LANES), bf16),
            vm(g.shape, bf16),
            dma((2,)),
            dma,
            dma,
            dma((16,)),
            dma((16,)),
            dma((8,)),
            dma((8,)),
            dma((3,)),
            dma((3,)),
            dma((16,)),
            dma((16,)),
            dma((16,)),
            dma((16,)),
        ],
        compiler_params=pltpu.CompilerParams(
            collective_id=0, has_side_effects=True, vmem_limit_bytes=32 << 20
        ),
    )(g)


def on_device(
    out_grad, pre_act, batch_count, layer_two, hot_slots, cold_index, hot_feats, cold_feats
):
    fanout = hot_slots.shape[1] + cold_index.shape[1]
    din, dh = hot_feats.shape[1], out_grad.shape[1]
    hot_all = lax.all_gather(hot_feats, "clique", axis=0, tiled=True)
    hot = hot_all.shape[0]
    slots = hot + cold_feats.shape[0]
    parts, grad_two = parts_call(
        fanout, out_grad, pre_act, batch_count, layer_two, hot_slots, cold_index, slots
    )
    grad_one = jnp.dot(hot_all.T, parts[:hot], preferred_element_type=jnp.float32)
    grad_one = grad_one + jnp.dot(
        cold_feats.T, parts[hot:], preferred_element_type=jnp.float32
    )
    both = jnp.concatenate([grad_one, grad_two], 0).astype(jnp.bfloat16)
    total = sum_call(both.reshape(-1, 8, dh)).reshape(-1, dh).astype(jnp.float32)
    return total[:din], total[din:]


def solution(mesh):
    placed = (
        P(("clique", "copy"), None),
        P(("clique", "copy"), None),
        P(("clique", "copy")),
        P(),
        P(("clique", "copy"), None),
        P(("clique", "copy"), None),
        P("clique", None),
        P(("clique", "copy"), None),
    )
    return jax.shard_map(
        on_device, mesh=mesh, in_specs=placed, out_specs=(P(), P()), check_vma=False
    )
```

```python
import functools
import jax
import jax.numpy as jnp
from jax import lax
from jax.experimental import pallas as pl
from jax.experimental.pallas import tpu as pltpu
from jax.sharding import PartitionSpec as P

MESH = pl.DeviceIdType.MESH
BLK = 512
WB = BLK // 8
LANES = 128


def build_counts(idx_ref, block, c_ref):
    k_n, rows = idx_ref.shape
    sub = lax.broadcasted_iota(jnp.int32, (8, LANES), 0)
    for j in range(rows // LANES):
        cols = slice(j * LANES, j * LANES + LANES)
        local = idx_ref[:, cols] - block * BLK
        inside = (local >= 0) & (local < BLK)
        word = jnp.where(inside, local & (WB - 1), -1)
        unit = jnp.left_shift(jnp.ones_like(local), ((local >> 6) & 7) * 4)
        ws = [jnp.broadcast_to(word[k : k + 1], (8, LANES)) for k in range(k_n)]
        us = [jnp.broadcast_to(unit[k : k + 1], (8, LANES)) for k in range(k_n)]
        for pair in range(WB // 16):
            two = []
            for h in range(2):
                at = sub + (pair * 16 + h * 8)
                acc = jnp.where(ws[0] == at, us[0], 0)
                for k in range(1, k_n):
                    acc = acc + jnp.where(ws[k] == at, us[k], 0)
                two.append(acc)
            words = jnp.concatenate(two, 0)
            for b in range(8):
                field = (words >> (4 * b)) & 15
                at = b * WB + pair * 16
                c_ref[at : at + 16, cols] = field.astype(jnp.float32).astype(jnp.bfloat16)


class Place:
    def __init__(self):
        clique, copy = lax.axis_index("clique"), lax.axis_index("copy")
        self.x, self.y = clique % 4, (clique // 4) * 2 + (copy // 2) % 2
        self.z, self.core = copy // 4, copy % 2
        self.member = self.x * 4 + self.y

    def device(self, x, y, z, core):
        return ((y // 2) * 4 + x, z * 4 + (y % 2) * 2 + core)

    def mate(self):
        return self.device(self.x, self.y, self.z, 1 - self.core)

    def plane(self):
        for dx in range(4):
            for dy in range(4):
                if dx or dy:
                    x, y = (self.x + dx) % 4, (self.y + dy) % 4
                    yield x * 4 + y, self.device(x, y, self.z, self.core)

    def column(self, steps):
        for dz in steps:
            z = (self.z + dz) % 8
            yield z, self.device(self.x, self.y, z, self.core)


def remote(src, dst, send, recv, device):
    return pltpu.make_async_remote_copy(
        src_ref=src, dst_ref=dst, send_sem=send, recv_sem=recv, device_id=device, device_id_type=MESH
    )


class Gather:
    def __init__(self, here, own, feats, send, recv):
        h, n = BLK // 2, iter(range(15))
        self.out, self.into, self.own = [], [], own
        right = here.device((here.x + 1) % 4, here.y, here.z, here.core)
        left = here.device((here.x + 3) % 4, here.y, here.z, here.core)
        across = here.device(here.x, 3 - here.y, here.z, here.core)
        hi = here.y // 2

        def rows(dx, flip, core, start=0, count=h):
            block = (1 - hi if flip else hi) * 4 + (here.x + dx) % 4
            return feats.at[pl.ds(pl.multiple_of(block * BLK + core * h + start, h // 2), count), :]

        def add(to, dx, flip, got_dx, got_flip, start=0, count=h, first=False):
            i = next(n)
            dst = rows(dx, flip, here.core, start, count)
            src = own.at[pl.ds(pl.multiple_of(here.core * h, h), h), :] if first else dst
            self.out.append(remote(src, dst, send.at[i], recv.at[i], to))
            core = here.core if to is not mate else 1 - here.core
            got = rows(got_dx, got_flip, core, start, count)
            self.into.append(remote(got, got, send.at[i], recv.at[i], to))

        mate = here.mate()
        q = h // 2
        add(right, 0, False, 3, False, first=True)
        add(left, 0, False, 1, False, first=True)
        add(across, 0, False, 0, True, first=True)
        add(right, 3, False, 2, False, 0, q)
        add(mate, 3, False, 3, False)
        add(left, 1, False, 2, False, q, q)
        add(mate, 1, False, 1, False)
        add(right, 0, True, 3, True)
        add(left, 0, True, 1, True)
        add(mate, 0, True, 0, True)
        add(across, 2, False, 2, True)
        add(mate, 2, False, 2, False)
        add(mate, 3, True, 3, True)
        add(mate, 1, True, 1, True)
        add(mate, 2, True, 2, True)

    def run(self, steps):
        for got, go in steps:
            for i in got:
                self.into[i].wait_recv()
            for i in go:
                self.out[i].start()

    def first(self):
        self.run([((), (0, 1, 2))])

    def second(self):
        self.run([((0,), (3,)), ((1,), (5,)), ((2,), (7, 8)), ((), (4, 6, 9))])

    def third(self):
        self.run([((3, 5), (10, 11)), ((7,), (12,)), ((8,), (13,))])

    def fourth(self):
        self.run([((10,), (14,)), ((4, 6, 9, 11, 12, 13, 14), ())])

    def finish(self):
        for c in self.out:
            c.wait_send()


class Sum:
    def __init__(self, here, bufs, sems):
        self.here = here
        self.g, self.rc, self.hs, self.ra, self.ms, self.rb, self.out = bufs
        c_s, c_r, a_s, a_r, b_s, b_r, d_s, d_r, e_s, e_r, f_s, f_r = sems
        g, rc, hs, ra, ms, rb, out = bufs
        half = rc.shape[0]
        per = half // 16
        mate, me = here.mate(), here.member
        plane = list(here.plane())
        column = list(here.column(range(1, 8)))
        self.mine, self.other = here.core * half, (1 - here.core) * half
        self.half, self.per = half, per
        self.swap = remote(g.at[pl.ds(self.other, half)], rc, c_s, c_r, mate)
        self.to_plane = [
            remote(hs.at[pl.ds(q * per, per)], ra.at[me], a_s.at[q], a_r.at[me], d) for q, d in plane
        ]
        self.of_plane = [
            remote(hs.at[pl.ds(q * per, per)], ra.at[q], a_s.at[q], a_r.at[q], d) for q, d in plane
        ]

        def block(z):
            return pl.ds(pl.multiple_of((z % 4) * LANES, LANES), LANES)

        self.part = part = block(here.z)
        self.to_column = [
            remote(ms.at[:, :, block(z)], rb.at[here.z], b_s.at[z], b_r.at[here.z], d) for z, d in column
        ]
        self.of_column = [
            remote(ms.at[:, :, part], rb.at[z], b_s.at[z], b_r.at[z], d) for z, d in column
        ]
        self.slot = slot = pl.ds(self.mine + me * per, per)
        steps = (1, 7, 6)
        mine = out.at[slot, :, part]
        self.back_to = [
            remote(mine, mine, d_s.at[n], d_r.at[n], d) for n, (z, d) in enumerate(here.column(steps))
        ]
        self.back_of = []
        for n, (z, d) in enumerate(here.column([8 - s for s in steps])):
            theirs = out.at[slot, :, block(z)]
            self.back_of.append(remote(theirs, theirs, d_s.at[n], d_r.at[n], d))
        self.home_to, self.home_of, self.pass_to, self.pass_of = [], [], [], []
        for q, d in plane:
            at = out.at[pl.ds(self.mine + q * per, per)]
            self.home_to.append(remote(out.at[slot], out.at[slot], e_s.at[q], e_r.at[me], d))
            self.home_of.append(remote(at, at, e_s.at[q], e_r.at[q], d))
            self.pass_to.append(remote(at, at, f_s.at[q], f_r.at[q], mate))
        self.own_to = remote(out.at[slot], out.at[slot], f_s.at[me], f_r.at[me], mate)
        for q in range(16):
            at = out.at[pl.ds(self.other + q * per, per)]
            self.pass_of.append(remote(at, at, f_s.at[q], f_r.at[q], mate))

    def to_pair(self):
        self.swap.start()

    def to_the_plane(self):
        f32 = jnp.float32
        self.swap.wait_recv()
        both = self.g[pl.ds(self.mine, self.half)].astype(f32) + self.rc[...].astype(f32)
        self.hs[...] = both.astype(jnp.bfloat16)
        for c in self.to_plane:
            c.start()
        self.ra[self.here.member] = self.hs[pl.ds(self.here.member * self.per, self.per)]

    def to_the_column(self):
        for c in self.of_plane:
            c.wait_recv()
        self.ms[...] = jnp.sum(self.ra[...].astype(jnp.float32), axis=0).astype(jnp.bfloat16)
        for c in self.to_column:
            c.start()
        self.rb[self.here.z] = self.ms[:, :, self.part]

    def back_in_column(self):
        for c in self.of_column:
            c.wait_recv()
        total = jnp.sum(self.rb[...].astype(jnp.float32), axis=0).astype(jnp.bfloat16)
        self.out[self.slot, :, self.part] = total
        for c in self.back_to:
            c.start()

    def back_in_plane(self):
        for c in self.back_of:
            c.wait_recv()
        for c in self.home_to:
            c.start()
        self.own_to.start()

    def back_to_pair(self):
        for c, then in zip(self.home_of, self.pass_to):
            c.wait_recv()
            then.start()

    def received(self):
        for c in self.pass_of:
            c.wait_recv()

    def finish(self):
        sent = [self.swap, *self.to_plane, *self.to_column, *self.back_to, *self.home_to, *self.pass_to]
        for c in [*sent, self.own_to]:
            c.wait_send()


def whole_kernel(
    fanout, cnt_ref, og_hbm, pa_hbm, l2_hbm, hs_hbm, ci_hbm, hf_hbm, cf_hbm, one_hbm, two_hbm,
    og, pa, l2, hs, ci, feats, rg, hp, c0, c1, two, sems, g_send, g_recv, one_bufs, one_sems, two_bufs, two_sems,
):
    rows, dh = og.shape
    din = feats.shape[1]
    tile = 512
    hot_n = hf_hbm.shape[0] * 8
    here = Place()
    gather = Gather(here, hf_hbm, feats, g_send, g_recv)
    sum_one = Sum(here, one_bufs, one_sems)
    sum_two = Sum(here, two_bufs, two_sems)
    home = pl.ds(pl.multiple_of(lax.axis_index("clique") * BLK, BLK), BLK)
    pairs = [
        (l2_hbm, l2),
        (og_hbm, og),
        (pa_hbm, pa),
        (ci_hbm, ci),
        (hs_hbm, hs),
        (cf_hbm, feats.at[pl.ds(hot_n, cf_hbm.shape[0]), :]),
        (hf_hbm, feats.at[home, :]),
    ]
    copies = [pltpu.make_async_copy(s, d, sems.at[i]) for i, (s, d) in enumerate(pairs)]
    barrier = pltpu.get_barrier_semaphore()
    peers = [here.mate()] + [d for _, d in here.plane()] + [d for _, d in here.column(range(1, 8))]
    for d in peers:
        pl.semaphore_signal(barrier, inc=1, device_id=d, device_id_type=MESH)
    for c in copies:
        c.start()
    pl.semaphore_wait(barrier, len(peers))
    gather.first()
    for c in copies[:3]:
        c.wait()
    count = cnt_ref[0]
    two[...] = jnp.zeros_like(two)

    def some_rows(i, carry):
        at = pl.ds(pl.multiple_of(i * tile, tile), tile)
        live = (lax.broadcasted_iota(jnp.int32, (tile, 1), 0) + i * tile) < count
        o = og[at, :]
        masked = jnp.where(live, o, jnp.zeros_like(o))
        p = pa[at, :]
        back = lax.dot_general(
            masked, l2[...], (((1,), (1,)), ((), ())), preferred_element_type=jnp.float32
        )
        rg[at, :] = jnp.where(p > 0, back, 0.0).astype(jnp.bfloat16)
        activ = jnp.maximum(p, jnp.zeros_like(p))
        two[...] += lax.dot_general(
            activ, masked, (((0,), (0,)), ((), ())), preferred_element_type=jnp.float32
        )
        return carry

    lax.fori_loop(0, rows // tile, some_rows, 0)
    sum_two.g[...] = two[...].reshape(dh // 8, 8, dh).astype(jnp.bfloat16)
    sum_two.to_pair()
    for c in copies[3:5]:
        c.wait()
    n_hot = hot_n // BLK

    def step(idx_ref, block, c_new, c_old, base):
        if idx_ref is not None:
            build_counts(idx_ref, block, c_new)
        p = jnp.dot(c_old[...], rg[...], preferred_element_type=jnp.float32)
        at = pl.ds(pl.multiple_of(base, BLK), BLK)
        hp[at, :] = (p * (1.0 / fanout)).astype(jnp.bfloat16)

    build_counts(ci, 0, c0)
    step(ci, 1, c1, c0, hot_n)
    sum_two.to_the_plane()
    step(ci, 2, c0, c1, hot_n + BLK)
    gather.second()
    step(ci, 3, c1, c0, hot_n + 2 * BLK)
    step(hs, 0, c0, c1, hot_n + 3 * BLK)
    sum_two.to_the_column()

    def hot(i, carry):
        step(hs, 2 * i + 1, c1, c0, 2 * i * BLK)
        step(hs, 2 * i + 2, c0, c1, (2 * i + 1) * BLK)

        @pl.when(i == 0)
        def _():
            sum_two.back_in_column()

        @pl.when(i == 1)
        def _():
            gather.third()
            sum_two.back_in_plane()

        @pl.when(i == 2)
        def _():
            sum_two.back_to_pair()

        return carry

    lax.fori_loop(0, n_hot // 2 - 1, hot, 0)
    step(hs, n_hot - 1, c1, c0, (n_hot - 2) * BLK)
    step(None, 0, c0, c1, (n_hot - 1) * BLK)
    sum_two.received()
    two_out = pltpu.make_async_copy(sum_two.out, two_hbm, sems.at[7])
    two_out.start()
    for c in copies[5:]:
        c.wait()
    gather.fourth()

    def some_sums(core):
        at = pl.ds(pl.multiple_of(core * (din // 2), LANES), din // 2)
        sums = lax.dot_general(
            feats[:, at], hp[...], (((0,), (0,)), ((), ())), preferred_element_type=jnp.float32
        )
        half = sum_one.half
        sum_one.g[pl.ds(core * half, half)] = sums.reshape(half, 8, dh).astype(jnp.bfloat16)

    some_sums(1 - here.core)
    sum_one.to_pair()
    some_sums(here.core)
    sum_one.to_the_plane()
    sum_one.to_the_column()
    sum_one.back_in_column()
    sum_one.back_in_plane()
    sum_one.back_to_pair()
    sum_one.received()
    one_out = pltpu.make_async_copy(sum_one.out, one_hbm, sems.at[8])
    one_out.start()
    gather.finish()
    sum_two.finish()
    sum_one.finish()
    two_out.wait()
    one_out.wait()


def sum_scratch(rows, dh):
    vm, dma, bf16 = pltpu.VMEM, pltpu.SemaphoreType.DMA, jnp.bfloat16
    units = rows // 8
    half, per = units // 2, units // 32
    bufs = (
        vm((units, 8, dh), bf16),
        vm((half, 8, dh), bf16),
        vm((half, 8, dh), bf16),
        vm((16, per, 8, dh), bf16),
        vm((per, 8, dh), bf16),
        vm((8, per, 8, LANES), bf16),
        vm((units, 8, dh), bf16),
    )
    sems = [dma, dma] + [dma((n,)) for n in (16, 16, 8, 8, 3, 3, 16, 16, 16, 16)]
    return bufs, tuple(sems)


def whole_call(fanout, og, pa, cnt, l2, hs, ci, hf, cf):
    vm, dma = pltpu.VMEM, pltpu.SemaphoreType.DMA
    hbm = pl.BlockSpec(memory_space=pltpu.HBM)
    bf16 = jnp.bfloat16
    rows, dh = og.shape
    din = hf.shape[1]
    slots = hf.shape[0] * 8 + cf.shape[0]
    one_bufs, one_sems = sum_scratch(din, dh)
    two_bufs, two_sems = sum_scratch(dh, dh)
    return pl.pallas_call(
        functools.partial(whole_kernel, fanout),
        out_shape=(
            jax.ShapeDtypeStruct((din // 8, 8, dh), bf16),
            jax.ShapeDtypeStruct((dh // 8, 8, dh), bf16),
        ),
        in_specs=[pl.BlockSpec(memory_space=pltpu.SMEM)] + [hbm] * 7,
        out_specs=[hbm] * 2,
        scratch_shapes=[
            vm((rows, dh), bf16),
            vm((rows, dh), bf16),
            vm((dh, dh), bf16),
            vm((hs.shape[1], rows), jnp.int32),
            vm((ci.shape[1], rows), jnp.int32),
            vm((slots, din), bf16),
            vm((rows, dh), bf16),
            vm((slots, dh), bf16),
            vm((BLK, rows), bf16),
            vm((BLK, rows), bf16),
            vm((dh, dh), jnp.float32),
            dma((9,)),
            dma((15,)),
            dma((15,)),
            one_bufs,
            one_sems,
            two_bufs,
            two_sems,
        ],
        compiler_params=pltpu.CompilerParams(
            collective_id=0, has_side_effects=True, vmem_limit_bytes=56 << 20
        ),
    )(cnt, og, pa, l2, hs.T, ci.T, hf, cf)


def on_device(
    out_grad, pre_act, batch_count, layer_two, hot_slots, cold_index, hot_feats, cold_feats
):
    fanout = hot_slots.shape[1] + cold_index.shape[1]
    one, two = whole_call(
        fanout, out_grad, pre_act, batch_count, layer_two, hot_slots, cold_index, hot_feats, cold_feats
    )
    dh = out_grad.shape[1]
    return one.reshape(-1, dh).astype(jnp.float32), two.reshape(-1, dh).astype(jnp.float32)


def solution(mesh):
    placed = (
        P(("clique", "copy"), None),
        P(("clique", "copy"), None),
        P(("clique", "copy")),
        P(),
        P(("clique", "copy"), None),
        P(("clique", "copy"), None),
        P("clique", None),
        P(("clique", "copy"), None),
    )
    return jax.shard_map(
        on_device, mesh=mesh, in_specs=placed, out_specs=(P(), P()), check_vma=False
    )
```

```python
import functools
import jax
import jax.numpy as jnp
from jax import lax
from jax.experimental import pallas as pl
from jax.experimental.pallas import tpu as pltpu
from jax.sharding import PartitionSpec as P

MESH = pl.DeviceIdType.MESH
BLK = 512
FIELDS = 16
WB = BLK // FIELDS
LANES = 128


def split_indices(idx_ref, unit_ref):
    idx = idx_ref[...]
    unit_ref[...] = jnp.left_shift(jnp.ones_like(idx), ((idx >> 5) & 15) * 2)
    idx_ref[...] = (idx >> 9) * WB + (idx & (WB - 1))


def build_counts(word_ref, unit_ref, block, c_ref):
    k_n, rows = word_ref.shape
    assert k_n <= 15
    sub = lax.broadcasted_iota(jnp.int32, (8, LANES), 0) + block * WB
    low = jnp.full((8, LANES), 0x33333333, jnp.int32)
    for j in range(rows // LANES):
        cols = slice(j * LANES, j * LANES + LANES)
        ws = [jnp.broadcast_to(word_ref[k : k + 1, cols], (8, LANES)) for k in range(k_n)]
        us = [jnp.broadcast_to(unit_ref[k : k + 1, cols], (8, LANES)) for k in range(k_n)]
        halves = ([], [])
        for t in range(WB // 8):
            at = sub + t * 8
            even, odd = [], []
            for first in range(0, k_n, 3):
                acc = None
                for k in range(first, min(first + 3, k_n)):
                    hit = jnp.where(ws[k] == at, us[k], 0)
                    acc = hit if acc is None else acc + hit
                even.append(acc & low)
                odd.append((acc >> 2) & low)
            halves[0].append(functools.reduce(lambda p, q: p + q, even))
            halves[1].append(functools.reduce(lambda p, q: p + q, odd))
        for parity in range(2):
            for t in range(0, WB // 8, 2):
                words = jnp.concatenate(halves[parity][t : t + 2], 0)
                for b in range(8):
                    if b < 7:
                        field = words & (15 << (4 * b))
                    else:
                        field = lax.shift_right_logical(words, jnp.full_like(words, 28))
                    at = (2 * b + parity) * WB + t * 8
                    c_ref[at : at + 16, cols] = field.astype(jnp.float32).astype(jnp.bfloat16)


def field_scale(b):
    return 2.0 ** (-4 * b) if b < 7 else 1.0


class Place:
    def __init__(self):
        clique, copy = lax.axis_index("clique"), lax.axis_index("copy")
        self.x, self.y = clique % 4, (clique // 4) * 2 + (copy // 2) % 2
        self.z, self.core = copy // 4, copy % 2
        self.member = self.x * 4 + self.y

    def device(self, x, y, z, core):
        return ((y // 2) * 4 + x, z * 4 + (y % 2) * 2 + core)

    def mate(self):
        return self.device(self.x, self.y, self.z, 1 - self.core)

    def plane(self):
        for dx in range(4):
            for dy in range(4):
                if dx or dy:
                    x, y = (self.x + dx) % 4, (self.y + dy) % 4
                    yield x * 4 + y, self.device(x, y, self.z, self.core)

    def column(self, steps):
        for dz in steps:
            z = (self.z + dz) % 8
            yield z, self.device(self.x, self.y, z, self.core)


def remote(src, dst, send, recv, device):
    return pltpu.make_async_remote_copy(
        src_ref=src, dst_ref=dst, send_sem=send, recv_sem=recv, device_id=device, device_id_type=MESH
    )


class Gather:
    def __init__(self, here, own, feats, send, recv):
        h, q, e = BLK // 2, BLK // 4, BLK // 8
        self.out, self.into = [], []
        right = here.device((here.x + 1) % 4, here.y, here.z, here.core)
        left = here.device((here.x + 3) % 4, here.y, here.z, here.core)
        across = here.device(here.x, 3 - here.y, here.z, here.core)
        up = here.device(here.x, here.y, (here.z + 1) % 8, here.core)
        down = here.device(here.x, here.y, (here.z + 7) % 8, here.core)
        mate = here.mate()
        hi = here.y // 2
        p = (here.z % 2) * q
        o = q - p

        def rows(piece, core):
            dx, flip, start, count = piece
            block = (1 - hi if flip else hi) * 4 + (here.x + dx) % 4
            return feats.at[pl.ds(pl.multiple_of(block * BLK + core * h + start, e), count), :]

        def add(to, piece, got, source=None):
            i = len(self.out)
            dst = rows(piece, here.core)
            self.out.append(remote(dst if source is None else source, dst, send.at[i], recv.at[i], to))
            land = rows(got, 1 - here.core if to is mate else here.core)
            self.into.append(remote(land, land, send.at[i], recv.at[i], to))

        mine = own.at[pl.ds(pl.multiple_of(here.core * h + p, e), q), :]
        N, F = False, True
        add(right, (0, N, p, q), (3, N, p, q), mine)
        add(left, (0, N, p, q), (1, N, p, q), mine)
        add(across, (0, N, p, q), (0, F, p, q), mine)
        add(right, (3, N, p, e), (2, N, p, e))
        add(left, (1, N, p + e, e), (2, N, p + e, e))
        add(right, (0, F, p, q), (3, F, p, q))
        add(left, (0, F, p, q), (1, F, p, q))
        add(up, (3, N, p, q), (3, N, o, q))
        add(down, (1, N, p, q), (1, N, o, q))
        add(up, (0, F, p, q), (0, F, o, q))
        for piece in ((3, N, p, q), (1, N, p, q), (0, F, p, q)):
            add(mate, piece, piece)
        add(across, (2, N, p, q), (2, F, p, q))
        add(down, (2, N, p, q), (2, N, o, q))
        add(up, (3, F, p, q), (3, F, o, q))
        add(down, (1, F, p, q), (1, F, o, q))
        for piece in ((2, N, p, q), (3, F, p, q), (1, F, p, q)):
            add(mate, piece, piece)
        add(up, (2, F, p, e), (2, F, o, e))
        add(down, (2, F, p + e, e), (2, F, o + e, e))
        add(mate, (2, F, p, q), (2, F, p, q))
        for piece in ((3, N, o, q), (1, N, o, q), (0, F, o, q)):
            add(mate, piece, piece)
        for piece in ((2, N, o, q), (3, F, o, q), (1, F, o, q), (2, F, o, q)):
            add(mate, piece, piece)

    def run(self, *steps):
        for got, go in steps:
            for i in got:
                self.into[i].wait_recv()
            for i in go:
                self.out[i].start()

    def first(self):
        self.run(((), (0, 1, 2)))

    def second(self):
        self.run(((2,), (5, 6, 9)), ((0,), (3, 7)), ((1,), (4, 8)), ((), (10, 11, 12)))

    def third(self):
        self.run(((3, 4), (13, 14)), ((5,), (15,)), ((6,), (16,)), ((), (17, 18, 19)))

    def fourth(self):
        self.run(((13,), (20, 21, 22)), ((7,), (23,)), ((8,), (24,)), ((9,), (25,)))

    def fifth(self):
        self.run(((14,), (26,)), ((15,), (27,)), ((16,), (28,)), ((20, 21), (29,)))

    def sixth(self):
        self.run(((10, 11, 12, 17, 18, 19, *range(22, 30)), ()))

    def finish(self):
        for c in self.out:
            c.wait_send()


class Sum:
    def __init__(self, here, bufs, sems):
        self.here = here
        self.g, self.rc, self.hs, self.ra, self.ms, self.rb, self.out = bufs
        c_s, c_r, a_s, a_r, b_s, b_r, d_s, d_r, e_s, e_r, f_s, f_r = sems
        g, rc, hs, ra, ms, rb, out = bufs
        half = rc.shape[0]
        per = half // 16
        mate, me = here.mate(), here.member
        plane = list(here.plane())
        column = list(here.column(range(1, 8)))
        self.mine, self.other = here.core * half, (1 - here.core) * half
        self.half, self.per = half, per
        self.swap = remote(g.at[pl.ds(self.other, half)], rc, c_s, c_r, mate)
        self.to_plane = [
            remote(hs.at[pl.ds(q * per, per)], ra.at[me], a_s.at[q], a_r.at[me], d) for q, d in plane
        ]
        self.of_plane = [
            remote(hs.at[pl.ds(q * per, per)], ra.at[q], a_s.at[q], a_r.at[q], d) for q, d in plane
        ]

        def block(z):
            return pl.ds(pl.multiple_of((z % 4) * LANES, LANES), LANES)

        self.part = part = block(here.z)
        self.to_column = [
            remote(ms.at[:, :, block(z)], rb.at[here.z], b_s.at[z], b_r.at[here.z], d) for z, d in column
        ]
        self.of_column = [
            remote(ms.at[:, :, part], rb.at[z], b_s.at[z], b_r.at[z], d) for z, d in column
        ]
        self.slot = slot = pl.ds(self.mine + me * per, per)
        steps = (1, 7, 6)
        mine = out.at[slot, :, part]
        self.back_to = [
            remote(mine, mine, d_s.at[n], d_r.at[n], d) for n, (z, d) in enumerate(here.column(steps))
        ]
        self.back_of = []
        for n, (z, d) in enumerate(here.column([8 - s for s in steps])):
            theirs = out.at[slot, :, block(z)]
            self.back_of.append(remote(theirs, theirs, d_s.at[n], d_r.at[n], d))
        self.home_to, self.home_of, self.pass_to, self.pass_of = [], [], [], []
        for q, d in plane:
            at = out.at[pl.ds(self.mine + q * per, per)]
            self.home_to.append(remote(out.at[slot], out.at[slot], e_s.at[q], e_r.at[me], d))
            self.home_of.append(remote(at, at, e_s.at[q], e_r.at[q], d))
            self.pass_to.append(remote(at, at, f_s.at[q], f_r.at[q], mate))
        self.own_to = remote(out.at[slot], out.at[slot], f_s.at[me], f_r.at[me], mate)
        for q in range(16):
            at = out.at[pl.ds(self.other + q * per, per)]
            self.pass_of.append(remote(at, at, f_s.at[q], f_r.at[q], mate))

    def to_pair(self):
        self.swap.start()

    def to_the_plane(self):
        f32 = jnp.float32
        self.swap.wait_recv()
        both = self.g[pl.ds(self.mine, self.half)].astype(f32) + self.rc[...].astype(f32)
        self.hs[...] = both.astype(jnp.bfloat16)
        for c in self.to_plane:
            c.start()
        self.ra[self.here.member] = self.hs[pl.ds(self.here.member * self.per, self.per)]

    def to_the_column(self):
        for c in self.of_plane:
            c.wait_recv()
        self.ms[...] = jnp.sum(self.ra[...].astype(jnp.float32), axis=0).astype(jnp.bfloat16)
        for c in self.to_column:
            c.start()
        self.rb[self.here.z] = self.ms[:, :, self.part]

    def back_in_column(self):
        for c in self.of_column:
            c.wait_recv()
        total = jnp.sum(self.rb[...].astype(jnp.float32), axis=0).astype(jnp.bfloat16)
        self.out[self.slot, :, self.part] = total
        for c in self.back_to:
            c.start()

    def back_in_plane(self):
        for c in self.back_of:
            c.wait_recv()
        for c in self.home_to:
            c.start()
        self.own_to.start()

    def back_to_pair(self):
        for c, then in zip(self.home_of, self.pass_to):
            c.wait_recv()
            then.start()

    def received(self):
        for c in self.pass_of:
            c.wait_recv()

    def finish(self):
        sent = [self.swap, *self.to_plane, *self.to_column, *self.back_to, *self.home_to, *self.pass_to]
        for c in [*sent, self.own_to]:
            c.wait_send()


def whole_kernel(
    fanout, cnt_ref, og_hbm, pa_hbm, l2_hbm, hs_hbm, ci_hbm, hf_hbm, cf_hbm, one_ref, two_ref,
    og, pa, l2, hs, ci, hu, cu, feats, rg, hp, c0, c1, acc, sems, g_send, g_recv, one_bufs, one_sems, two_bufs, two_sems,
):
    rows, dh = og.shape
    din = feats.shape[1]
    tile = 512
    hot_n = hf_hbm.shape[0] * 8
    here = Place()
    gather = Gather(here, hf_hbm, feats, g_send, g_recv)
    sum_one = Sum(here, one_bufs, one_sems)
    sum_two = Sum(here, two_bufs, two_sems)
    home = pl.ds(pl.multiple_of(lax.axis_index("clique") * BLK, BLK), BLK)
    pairs = [
        (l2_hbm, l2),
        (og_hbm, og),
        (pa_hbm, pa),
        (ci_hbm, ci),
        (hs_hbm, hs),
        (cf_hbm, feats.at[pl.ds(hot_n, cf_hbm.shape[0]), :]),
        (hf_hbm, feats.at[home, :]),
    ]
    copies = [pltpu.make_async_copy(s, d, sems.at[i]) for i, (s, d) in enumerate(pairs)]
    barrier = pltpu.get_barrier_semaphore()
    peers = [here.mate()] + [d for _, d in here.plane()] + [d for _, d in here.column(range(1, 8))]
    for d in peers:
        pl.semaphore_signal(barrier, inc=1, device_id=d, device_id_type=MESH)
    for c in copies:
        c.start()
    pl.semaphore_wait(barrier, len(peers))
    gather.first()
    for c in copies[:3]:
        c.wait()
    count = cnt_ref[0]
    acc[:dh, :] = jnp.zeros((dh, dh), jnp.float32)

    def some_rows(i, carry):
        at = pl.ds(pl.multiple_of(i * tile, tile), tile)
        live = (lax.broadcasted_iota(jnp.int32, (tile, 1), 0) + i * tile) < count
        o = og[at, :]
        masked = jnp.where(live, o, jnp.zeros_like(o))
        p = pa[at, :]
        back = lax.dot_general(
            masked, l2[...], (((1,), (1,)), ((), ())), preferred_element_type=jnp.float32
        )
        rg[at, :] = jnp.where(p > 0, back, 0.0).astype(jnp.bfloat16)
        activ = jnp.maximum(p, jnp.zeros_like(p))
        acc[:dh, :] += lax.dot_general(
            activ, masked, (((0,), (0,)), ((), ())), preferred_element_type=jnp.float32
        )
        return carry

    lax.fori_loop(0, rows // tile, some_rows, 0)
    sum_two.g[...] = acc[:dh, :].reshape(dh // 8, 8, dh).astype(jnp.bfloat16)
    sum_two.to_pair()
    for c in copies[3:5]:
        c.wait()
    split_indices(ci, cu)
    split_indices(hs, hu)
    n_hot = hot_n // BLK

    def step(refs, block, c_new, c_old, base):
        if refs is not None:
            build_counts(*refs, block, c_new)
        p = jnp.dot(c_old[...], rg[...], preferred_element_type=jnp.float32)
        size = BLK // 8
        for b in range(8):
            at = pl.ds(pl.multiple_of(base + b * size, size), size)
            scaled = p[b * size : b * size + size] * (field_scale(b) / fanout)
            hp[at, :] = scaled.astype(jnp.bfloat16)

    cold, warm = (ci, cu), (hs, hu)
    build_counts(*cold, 0, c0)
    gather.second()
    step(cold, 1, c1, c0, hot_n)
    step(cold, 2, c0, c1, hot_n + BLK)
    sum_two.to_the_plane()
    step(cold, 3, c1, c0, hot_n + 2 * BLK)
    step(warm, 0, c0, c1, hot_n + 3 * BLK)

    def hot(i, carry):
        step(warm, 2 * i + 1, c1, c0, 2 * i * BLK)
        step(warm, 2 * i + 2, c0, c1, (2 * i + 1) * BLK)

        @pl.when(i == 0)
        def _():
            gather.third()

        @pl.when(i == 1)
        def _():
            sum_two.to_the_column()

        @pl.when(i == 2)
        def _():
            gather.fourth()
            sum_two.back_in_column()

        return carry

    lax.fori_loop(0, n_hot // 2 - 1, hot, 0)
    step(warm, n_hot - 1, c1, c0, (n_hot - 2) * BLK)
    step(None, 0, c0, c1, (n_hot - 1) * BLK)
    for c in copies[5:]:
        c.wait()
    gather.fifth()
    sum_two.back_in_plane()
    turned = (((0,), (0,)), ((), ()))
    acc[...] = lax.dot_general(
        feats[hot_n:, :], hp[hot_n:, :], turned, preferred_element_type=jnp.float32
    )
    gather.sixth()

    def some_sums(core):
        width, half = din // 2, sum_one.half
        at = pl.ds(pl.multiple_of(core * width, LANES), width)
        sums = lax.dot_general(
            feats[:hot_n, at], hp[:hot_n, :], turned, preferred_element_type=jnp.float32
        )
        sums = sums + acc[at, :]
        sum_one.g[pl.ds(core * half, half)] = sums.reshape(half, 8, dh).astype(jnp.bfloat16)

    some_sums(1 - here.core)
    sum_one.to_pair()
    some_sums(here.core)
    sum_one.to_the_plane()
    sum_two.back_to_pair()
    sum_one.to_the_column()
    sum_two.received()
    two_ref[...] = sum_two.out[...]
    sum_one.back_in_column()
    sum_one.back_in_plane()
    sum_one.back_to_pair()
    sum_one.received()
    one_ref[...] = sum_one.out[...]
    gather.finish()
    sum_two.finish()
    sum_one.finish()


def sum_scratch(rows, dh):
    vm, dma, bf16 = pltpu.VMEM, pltpu.SemaphoreType.DMA, jnp.bfloat16
    units = rows // 8
    half, per = units // 2, units // 32
    bufs = (
        vm((units, 8, dh), bf16),
        vm((half, 8, dh), bf16),
        vm((half, 8, dh), bf16),
        vm((16, per, 8, dh), bf16),
        vm((per, 8, dh), bf16),
        vm((8, per, 8, LANES), bf16),
        vm((units, 8, dh), bf16),
    )
    sems = [dma, dma] + [dma((n,)) for n in (16, 16, 8, 8, 3, 3, 16, 16, 16, 16)]
    return bufs, tuple(sems)


def whole_call(fanout, og, pa, cnt, l2, hs, ci, hf, cf):
    vm, dma = pltpu.VMEM, pltpu.SemaphoreType.DMA
    hbm = pl.BlockSpec(memory_space=pltpu.HBM)
    bf16 = jnp.bfloat16
    rows, dh = og.shape
    din = hf.shape[1]
    slots = hf.shape[0] * 8 + cf.shape[0]
    one_bufs, one_sems = sum_scratch(din, dh)
    two_bufs, two_sems = sum_scratch(dh, dh)
    return pl.pallas_call(
        functools.partial(whole_kernel, fanout),
        out_shape=(
            jax.ShapeDtypeStruct((din // 8, 8, dh), bf16),
            jax.ShapeDtypeStruct((dh // 8, 8, dh), bf16),
        ),
        in_specs=[pl.BlockSpec(memory_space=pltpu.SMEM)] + [hbm] * 7,
        out_specs=[pl.BlockSpec(memory_space=vm)] * 2,
        scratch_shapes=[
            vm((rows, dh), bf16),
            vm((rows, dh), bf16),
            vm((dh, dh), bf16),
            vm((hs.shape[1], rows), jnp.int32),
            vm((ci.shape[1], rows), jnp.int32),
            vm((hs.shape[1], rows), jnp.int32),
            vm((ci.shape[1], rows), jnp.int32),
            vm((slots, din), bf16),
            vm((rows, dh), bf16),
            vm((slots, dh), bf16),
            vm((BLK, rows), bf16),
            vm((BLK, rows), bf16),
            vm((din, dh), jnp.float32),
            dma((7,)),
            dma((30,)),
            dma((30,)),
            one_bufs,
            one_sems,
            two_bufs,
            two_sems,
        ],
        compiler_params=pltpu.CompilerParams(
            collective_id=0, has_side_effects=True, vmem_limit_bytes=58 << 20
        ),
    )(cnt, og, pa, l2, hs.T, ci.T, hf, cf)


def on_device(
    out_grad, pre_act, batch_count, layer_two, hot_slots, cold_index, hot_feats, cold_feats
):
    fanout = hot_slots.shape[1] + cold_index.shape[1]
    one, two = whole_call(
        fanout, out_grad, pre_act, batch_count, layer_two, hot_slots, cold_index, hot_feats, cold_feats
    )
    dh = out_grad.shape[1]
    return one.reshape(-1, dh).astype(jnp.float32), two.reshape(-1, dh).astype(jnp.float32)


def solution(mesh):
    placed = (
        P(("clique", "copy"), None),
        P(("clique", "copy"), None),
        P(("clique", "copy")),
        P(),
        P(("clique", "copy"), None),
        P(("clique", "copy"), None),
        P("clique", None),
        P(("clique", "copy"), None),
    )
    return jax.shard_map(
        on_device, mesh=mesh, in_specs=placed, out_specs=(P(), P()), check_vma=False
    )
```

```python
import functools
import jax
import jax.numpy as jnp
from jax import lax
from jax.experimental import pallas as pl
from jax.experimental.pallas import tpu as pltpu
from jax.sharding import PartitionSpec as P

MESH = pl.DeviceIdType.MESH
BLK = 512
FIELDS = 16
WB = BLK // FIELDS
LANES = 128


def split_indices(idx_ref, unit_ref):
    idx = idx_ref[...]
    unit_ref[...] = jnp.left_shift(jnp.ones_like(idx), ((idx >> 5) & 15) * 2)
    idx_ref[...] = (idx >> 9) * WB + (idx & (WB - 1))


def build_counts(word_ref, unit_ref, block, c_ref):
    k_n, rows = word_ref.shape
    assert k_n <= 15
    sub = lax.broadcasted_iota(jnp.int32, (8, LANES), 0) + block * WB
    low = jnp.full((8, LANES), 0x33333333, jnp.int32)
    for j in range(rows // LANES):
        cols = slice(j * LANES, j * LANES + LANES)
        ws = [jnp.broadcast_to(word_ref[k : k + 1, cols], (8, LANES)) for k in range(k_n)]
        us = [jnp.broadcast_to(unit_ref[k : k + 1, cols], (8, LANES)) for k in range(k_n)]
        halves = ([], [])
        for t in range(WB // 8):
            at = sub + t * 8
            even, odd = [], []
            for first in range(0, k_n, 3):
                acc = None
                for k in range(first, min(first + 3, k_n)):
                    hit = jnp.where(ws[k] == at, us[k], 0)
                    acc = hit if acc is None else acc + hit
                even.append(acc & low)
                odd.append((acc >> 2) & low)
            halves[0].append(functools.reduce(lambda p, q: p + q, even))
            halves[1].append(functools.reduce(lambda p, q: p + q, odd))
        for parity in range(2):
            for t in range(0, WB // 8, 2):
                words = jnp.concatenate(halves[parity][t : t + 2], 0)
                for b in range(8):
                    if b < 7:
                        field = words & (15 << (4 * b))
                    else:
                        field = lax.shift_right_logical(words, jnp.full_like(words, 28))
                    at = (2 * b + parity) * WB + t * 8
                    c_ref[at : at + 16, cols] = field.astype(jnp.float32).astype(jnp.bfloat16)


def field_scale(b):
    return 2.0 ** (-4 * b) if b < 7 else 1.0


class Place:
    def __init__(self):
        clique, copy = lax.axis_index("clique"), lax.axis_index("copy")
        self.x, self.y = clique % 4, (clique // 4) * 2 + (copy // 2) % 2
        self.z, self.core = copy // 4, copy % 2
        self.member = self.x * 4 + self.y

    def device(self, x, y, z, core):
        return ((y // 2) * 4 + x, z * 4 + (y % 2) * 2 + core)

    def mate(self):
        return self.device(self.x, self.y, self.z, 1 - self.core)

    def plane(self):
        for dx in range(4):
            for dy in range(4):
                if dx or dy:
                    x, y = (self.x + dx) % 4, (self.y + dy) % 4
                    yield x * 4 + y, self.device(x, y, self.z, self.core)

    def column(self, steps):
        for dz in steps:
            z = (self.z + dz) % 8
            yield z, self.device(self.x, self.y, z, self.core)


def remote(src, dst, send, recv, device):
    return pltpu.make_async_remote_copy(
        src_ref=src, dst_ref=dst, send_sem=send, recv_sem=recv, device_id=device, device_id_type=MESH
    )


class Gather:
    def __init__(self, here, own, feats, send, recv):
        h, q, e = BLK // 2, BLK // 4, BLK // 8
        self.out, self.into = [], []
        right = here.device((here.x + 1) % 4, here.y, here.z, here.core)
        left = here.device((here.x + 3) % 4, here.y, here.z, here.core)
        across = here.device(here.x, 3 - here.y, here.z, here.core)
        up = here.device(here.x, here.y, (here.z + 1) % 8, here.core)
        down = here.device(here.x, here.y, (here.z + 7) % 8, here.core)
        mate = here.mate()
        hi = here.y // 2
        p = (here.z % 2) * q
        o = q - p

        def rows(piece, core):
            dx, flip, start, count = piece
            block = (1 - hi if flip else hi) * 4 + (here.x + dx) % 4
            return feats.at[pl.ds(pl.multiple_of(block * BLK + core * h + start, 16), count), :]

        def add(to, piece, got, source=None):
            i = len(self.out)
            dst = rows(piece, here.core)
            self.out.append(remote(dst if source is None else source, dst, send.at[i], recv.at[i], to))
            land = rows(got, 1 - here.core if to is mate else here.core)
            self.into.append(remote(land, land, send.at[i], recv.at[i], to))

        mine = own.at[pl.ds(pl.multiple_of(here.core * h + p, e), q), :]
        N, F = False, True
        add(right, (0, N, p, q), (3, N, p, q), mine)
        add(left, (0, N, p, q), (1, N, p, q), mine)
        add(across, (0, N, p, q), (0, F, p, q), mine)
        add(right, (3, N, p, e), (2, N, p, e))
        add(left, (1, N, p + e, e), (2, N, p + e, e))
        add(right, (0, F, p, q), (3, F, p, q))
        add(left, (0, F, p, q), (1, F, p, q))
        add(up, (3, N, p, q), (3, N, o, q))
        add(down, (1, N, p, q), (1, N, o, q))
        add(up, (0, F, p, q), (0, F, o, q))
        for piece in ((3, N, p, q), (1, N, p, q), (0, F, p, q)):
            add(mate, piece, piece)
        add(across, (2, N, p + 80, 48), (2, F, p + 80, 48))
        add(down, (2, N, p, q), (2, N, o, q))
        add(up, (3, F, p, q), (3, F, o, q))
        add(down, (1, F, p, q), (1, F, o, q))
        for piece in ((2, N, p, q), (3, F, p, q), (1, F, p, q)):
            add(mate, piece, piece)
        add(up, (2, F, p, e), (2, F, o, e))
        add(down, (2, F, p + e, e), (2, F, o + e, e))
        add(mate, (2, F, p, q), (2, F, p, q))
        for piece in ((3, N, o, q), (1, N, o, q), (0, F, o, q)):
            add(mate, piece, piece)
        for piece in ((2, N, o, q), (3, F, o, q), (1, F, o, q), (2, F, o, q)):
            add(mate, piece, piece)
        add(right, (3, F, p, 48), (2, F, p, 48))
        add(left, (1, F, p + 48, 32), (2, F, p + 48, 32))

    def run(self, *steps):
        for got, go in steps:
            for i in got:
                self.into[i].wait_recv()
            for i in go:
                self.out[i].start()

    def first(self):
        self.run(((), (0, 1, 2)))

    def second(self):
        self.run(((0,), (3,)), ((1,), (4,)), ((2,), (5, 6, 9, 7, 8)), ((), (10, 11, 12)))

    def third(self):
        self.run(((3, 4), (13, 14, 17)))

    def third_across(self):
        self.run(((5,), (30, 15)), ((6,), (31, 16)), ((), (18, 19)), ((7,), (23,)), ((8,), (24,)), ((9,), (25,)))

    def fourth(self):
        self.run(((13, 30, 31), (20, 21, 22)))

    def fifth(self):
        self.run(((14,), (26,)), ((15,), (27,)), ((16,), (28,)), ((20, 21), (29,)))

    def sixth(self):
        self.run(((10, 11, 12, 17, 18, 19, *range(22, 30)), ()))

    def finish(self):
        for c in self.out:
            c.wait_send()


class Sum:
    def __init__(self, here, bufs, sems):
        self.here = here
        self.g, self.rc, self.hs, self.ra, self.ms, self.rb, self.out = bufs
        c_s, c_r, a_s, a_r, b_s, b_r, d_s, d_r, e_s, e_r, f_s, f_r = sems
        g, rc, hs, ra, ms, rb, out = bufs
        half = rc.shape[0]
        per = half // 16
        mate, me = here.mate(), here.member
        plane = list(here.plane())
        column = list(here.column(range(1, 8)))
        self.mine, self.other = here.core * half, (1 - here.core) * half
        self.half, self.per = half, per
        self.swap = remote(g.at[pl.ds(self.other, half)], rc, c_s, c_r, mate)
        self.to_plane = [
            remote(hs.at[pl.ds(q * per, per)], ra.at[me], a_s.at[q], a_r.at[me], d) for q, d in plane
        ]
        self.of_plane = [
            remote(hs.at[pl.ds(q * per, per)], ra.at[q], a_s.at[q], a_r.at[q], d) for q, d in plane
        ]

        def block(z):
            return pl.ds(pl.multiple_of((z % 4) * LANES, LANES), LANES)

        self.part = part = block(here.z)
        self.to_column = [
            remote(ms.at[:, :, block(z)], rb.at[here.z], b_s.at[z], b_r.at[here.z], d) for z, d in column
        ]
        self.of_column = [
            remote(ms.at[:, :, part], rb.at[z], b_s.at[z], b_r.at[z], d) for z, d in column
        ]
        self.slot = slot = pl.ds(self.mine + me * per, per)
        steps = (1, 7, 6)
        mine = out.at[slot, :, part]
        self.back_to = [
            remote(mine, mine, d_s.at[n], d_r.at[n], d) for n, (z, d) in enumerate(here.column(steps))
        ]
        self.back_of = []
        for n, (z, d) in enumerate(here.column([8 - s for s in steps])):
            theirs = out.at[slot, :, block(z)]
            self.back_of.append(remote(theirs, theirs, d_s.at[n], d_r.at[n], d))
        self.home_to, self.home_of, self.pass_to, self.pass_of = [], [], [], []
        for q, d in plane:
            at = out.at[pl.ds(self.mine + q * per, per)]
            self.home_to.append(remote(out.at[slot], out.at[slot], e_s.at[q], e_r.at[me], d))
            self.home_of.append(remote(at, at, e_s.at[q], e_r.at[q], d))
            self.pass_to.append(remote(at, at, f_s.at[q], f_r.at[q], mate))
        self.own_to = remote(out.at[slot], out.at[slot], f_s.at[me], f_r.at[me], mate)
        for q in range(16):
            at = out.at[pl.ds(self.other + q * per, per)]
            self.pass_of.append(remote(at, at, f_s.at[q], f_r.at[q], mate))

    def to_pair(self):
        self.swap.start()

    def to_the_plane(self):
        f32 = jnp.float32
        self.swap.wait_recv()
        both = self.g[pl.ds(self.mine, self.half)].astype(f32) + self.rc[...].astype(f32)
        self.hs[...] = both.astype(jnp.bfloat16)
        for c in self.to_plane:
            c.start()
        self.ra[self.here.member] = self.hs[pl.ds(self.here.member * self.per, self.per)]

    def to_the_column(self):
        for c in self.of_plane:
            c.wait_recv()
        self.ms[...] = jnp.sum(self.ra[...].astype(jnp.float32), axis=0).astype(jnp.bfloat16)
        for c in self.to_column:
            c.start()
        self.rb[self.here.z] = self.ms[:, :, self.part]

    def back_in_column(self):
        for c in self.of_column:
            c.wait_recv()
        total = jnp.sum(self.rb[...].astype(jnp.float32), axis=0).astype(jnp.bfloat16)
        self.out[self.slot, :, self.part] = total
        for c in self.back_to:
            c.start()

    def back_in_plane(self):
        for c in self.back_of:
            c.wait_recv()
        for c in self.home_to:
            c.start()
        self.own_to.start()

    def back_to_pair(self):
        for c, then in zip(self.home_of, self.pass_to):
            c.wait_recv()
            then.start()

    def received(self):
        for c in self.pass_of:
            c.wait_recv()

    def finish(self):
        sent = [self.swap, *self.to_plane, *self.to_column, *self.back_to, *self.home_to, *self.pass_to]
        for c in [*sent, self.own_to]:
            c.wait_send()


def whole_kernel(
    fanout, cnt_ref, og_hbm, pa_hbm, l2_hbm, hs_hbm, ci_hbm, hf_hbm, cf_hbm, one_ref, two_ref,
    og, pa, l2, hs, ci, hu, cu, feats, rg, hp, c0, c1, acc, sems, g_send, g_recv, one_bufs, one_sems, two_bufs, two_sems,
):
    rows, dh = og.shape
    din = feats.shape[1]
    tile = 512
    hot_n = hf_hbm.shape[0] * 8
    here = Place()
    gather = Gather(here, hf_hbm, feats, g_send, g_recv)
    sums_one = [Sum(here, b, m) for b, m in zip(one_bufs, one_sems)]
    sum_two = Sum(here, two_bufs, two_sems)
    home = pl.ds(pl.multiple_of(lax.axis_index("clique") * BLK, BLK), BLK)
    pairs = [
        (l2_hbm, l2),
        (og_hbm, og),
        (pa_hbm, pa),
        (ci_hbm, ci),
        (hs_hbm, hs),
        (cf_hbm, feats.at[pl.ds(hot_n, cf_hbm.shape[0]), :]),
        (hf_hbm, feats.at[home, :]),
    ]
    copies = [pltpu.make_async_copy(s, d, sems.at[i]) for i, (s, d) in enumerate(pairs)]
    barrier = pltpu.get_barrier_semaphore()
    peers = [here.mate()] + [d for _, d in here.plane()] + [d for _, d in here.column(range(1, 8))]
    for d in peers:
        pl.semaphore_signal(barrier, inc=1, device_id=d, device_id_type=MESH)
    for c in copies:
        c.start()
    pl.semaphore_wait(barrier, len(peers))
    gather.first()
    for c in copies[:3]:
        c.wait()
    count = cnt_ref[0]
    acc[:dh, :] = jnp.zeros((dh, dh), jnp.float32)

    def some_rows(i, carry):
        at = pl.ds(pl.multiple_of(i * tile, tile), tile)
        live = (lax.broadcasted_iota(jnp.int32, (tile, 1), 0) + i * tile) < count
        o = og[at, :]
        masked = jnp.where(live, o, jnp.zeros_like(o))
        p = pa[at, :]
        back = lax.dot_general(
            masked, l2[...], (((1,), (1,)), ((), ())), preferred_element_type=jnp.float32
        )
        rg[at, :] = jnp.where(p > 0, back, 0.0).astype(jnp.bfloat16)
        activ = jnp.maximum(p, jnp.zeros_like(p))
        acc[:dh, :] += lax.dot_general(
            activ, masked, (((0,), (0,)), ((), ())), preferred_element_type=jnp.float32
        )
        return carry

    lax.fori_loop(0, rows // tile, some_rows, 0)
    sum_two.g[...] = acc[:dh, :].reshape(dh // 8, 8, dh).astype(jnp.bfloat16)
    sum_two.to_pair()
    for c in copies[3:5]:
        c.wait()
    split_indices(ci, cu)
    split_indices(hs, hu)
    n_hot = hot_n // BLK

    def step(refs, block, c_new, c_old, base):
        if refs is not None:
            build_counts(*refs, block, c_new)
        p = jnp.dot(c_old[...], rg[...], preferred_element_type=jnp.float32)
        size = BLK // 8
        for b in range(8):
            at = pl.ds(pl.multiple_of(base + b * size, size), size)
            scaled = p[b * size : b * size + size] * (field_scale(b) / fanout)
            hp[at, :] = scaled.astype(jnp.bfloat16)

    cold, warm = (ci, cu), (hs, hu)
    build_counts(*cold, 0, c0)
    step(cold, 1, c1, c0, hot_n)
    gather.second()
    step(cold, 2, c0, c1, hot_n + BLK)
    step(cold, 3, c1, c0, hot_n + 2 * BLK)
    step(warm, 0, c0, c1, hot_n + 3 * BLK)

    def hot(i, carry):
        step(warm, 2 * i + 1, c1, c0, 2 * i * BLK)
        step(warm, 2 * i + 2, c0, c1, (2 * i + 1) * BLK)

        @pl.when(i == 0)
        def _():
            gather.third()

        @pl.when(i == 1)
        def _():
            gather.third_across()

        return carry

    lax.fori_loop(0, n_hot // 2 - 1, hot, 0)
    step(warm, n_hot - 1, c1, c0, (n_hot - 2) * BLK)
    gather.fourth()
    sum_two.to_the_plane()
    step(None, 0, c0, c1, (n_hot - 1) * BLK)
    for c in copies[5:]:
        c.wait()
    turned = (((0,), (0,)), ((), ()))
    acc[...] = lax.dot_general(
        feats[hot_n:, :], hp[hot_n:, :], turned, preferred_element_type=jnp.float32
    )
    gather.fifth()
    gather.sixth()
    width = din // len(sums_one)

    def some_sums(n):
        at = slice(n * width, n * width + width)
        sums = acc[at, :] + lax.dot_general(
            feats[:hot_n, at], hp[:hot_n, :], turned, preferred_element_type=jnp.float32
        )
        sums_one[n].g[...] = sums.reshape(width // 8, 8, dh).astype(jnp.bfloat16)
        sums_one[n].to_pair()

    some_sums(0)
    some_sums(1)
    sums_one[0].to_the_plane()
    sum_two.to_the_column()
    some_sums(2)
    sums_one[1].to_the_plane()
    sums_one[2].to_the_plane()
    sum_two.back_in_column()
    for one in sums_one:
        one.to_the_column()
    sum_two.back_in_plane()
    for one in sums_one:
        one.back_in_column()
    for one in sums_one:
        one.back_in_plane()
    sum_two.back_to_pair()
    sum_two.received()
    two_ref[...] = sum_two.out[...]
    for n, one in enumerate(sums_one):
        one.back_to_pair()
    for n, one in enumerate(sums_one):
        one.received()
        one_ref[n * width // 8 : (n + 1) * width // 8] = one.out[...]
    gather.finish()
    sum_two.finish()
    for one in sums_one:
        one.finish()


def sum_scratch(rows, dh):
    vm, dma, bf16 = pltpu.VMEM, pltpu.SemaphoreType.DMA, jnp.bfloat16
    units = rows // 8
    half, per = units // 2, units // 32
    bufs = (
        vm((units, 8, dh), bf16),
        vm((half, 8, dh), bf16),
        vm((half, 8, dh), bf16),
        vm((16, per, 8, dh), bf16),
        vm((per, 8, dh), bf16),
        vm((8, per, 8, LANES), bf16),
        vm((units, 8, dh), bf16),
    )
    sems = [dma, dma] + [dma((n,)) for n in (16, 16, 8, 8, 3, 3, 16, 16, 16, 16)]
    return bufs, tuple(sems)


def whole_call(fanout, og, pa, cnt, l2, hs, ci, hf, cf):
    vm, dma = pltpu.VMEM, pltpu.SemaphoreType.DMA
    hbm = pl.BlockSpec(memory_space=pltpu.HBM)
    bf16 = jnp.bfloat16
    rows, dh = og.shape
    din = hf.shape[1]
    slots = hf.shape[0] * 8 + cf.shape[0]
    chunks = [sum_scratch(din // 3, dh) for _ in range(3)]
    one_bufs, one_sems = tuple(c[0] for c in chunks), tuple(c[1] for c in chunks)
    two_bufs, two_sems = sum_scratch(dh, dh)
    return pl.pallas_call(
        functools.partial(whole_kernel, fanout),
        out_shape=(
            jax.ShapeDtypeStruct((din // 8, 8, dh), bf16),
            jax.ShapeDtypeStruct((dh // 8, 8, dh), bf16),
        ),
        in_specs=[pl.BlockSpec(memory_space=pltpu.SMEM)] + [hbm] * 7,
        out_specs=[pl.BlockSpec(memory_space=vm)] * 2,
        scratch_shapes=[
            vm((rows, dh), bf16),
            vm((rows, dh), bf16),
            vm((dh, dh), bf16),
            vm((hs.shape[1], rows), jnp.int32),
            vm((ci.shape[1], rows), jnp.int32),
            vm((hs.shape[1], rows), jnp.int32),
            vm((ci.shape[1], rows), jnp.int32),
            vm((slots, din), bf16),
            vm((rows, dh), bf16),
            vm((slots, dh), bf16),
            vm((BLK, rows), bf16),
            vm((BLK, rows), bf16),
            vm((din, dh), jnp.float32),
            dma((7,)),
            dma((32,)),
            dma((32,)),
            one_bufs,
            one_sems,
            two_bufs,
            two_sems,
        ],
        compiler_params=pltpu.CompilerParams(
            collective_id=0, has_side_effects=True, vmem_limit_bytes=58 << 20
        ),
    )(cnt, og, pa, l2, hs.T, ci.T, hf, cf)


def on_device(
    out_grad, pre_act, batch_count, layer_two, hot_slots, cold_index, hot_feats, cold_feats
):
    fanout = hot_slots.shape[1] + cold_index.shape[1]
    one, two = whole_call(
        fanout, out_grad, pre_act, batch_count, layer_two, hot_slots, cold_index, hot_feats, cold_feats
    )
    dh = out_grad.shape[1]
    return one.reshape(-1, dh).astype(jnp.float32), two.reshape(-1, dh).astype(jnp.float32)


def solution(mesh):
    placed = (
        P(("clique", "copy"), None),
        P(("clique", "copy"), None),
        P(("clique", "copy")),
        P(),
        P(("clique", "copy"), None),
        P(("clique", "copy"), None),
        P("clique", None),
        P(("clique", "copy"), None),
    )
    return jax.shard_map(
        on_device, mesh=mesh, in_specs=placed, out_specs=(P(), P()), check_vma=False
    )
```

```python
import functools
import jax
import jax.numpy as jnp
from jax import lax
from jax.experimental import pallas as pl
from jax.experimental.pallas import tpu as pltpu
from jax.sharding import PartitionSpec as P

MESH = pl.DeviceIdType.MESH
BLK = 512
FIELDS = 16
WB = BLK // FIELDS
LANES = 128


def split_indices(idx_ref, unit_ref):
    idx = idx_ref[...]
    unit_ref[...] = jnp.left_shift(jnp.ones_like(idx), ((idx >> 5) & 15) * 2)
    idx_ref[...] = (idx >> 9) * WB + (idx & (WB - 1))


def build_counts(word_ref, unit_ref, block, c_ref):
    k_n, rows = word_ref.shape
    assert k_n <= 15
    sub = lax.broadcasted_iota(jnp.int32, (8, LANES), 0) + block * WB
    low = jnp.full((8, LANES), 0x33333333, jnp.int32)
    for j in range(rows // LANES):
        cols = slice(j * LANES, j * LANES + LANES)
        ws = [jnp.broadcast_to(word_ref[k : k + 1, cols], (8, LANES)) for k in range(k_n)]
        us = [jnp.broadcast_to(unit_ref[k : k + 1, cols], (8, LANES)) for k in range(k_n)]
        halves = ([], [])
        for t in range(WB // 8):
            at = sub + t * 8
            even, odd = [], []
            for first in range(0, k_n, 3):
                acc = None
                for k in range(first, min(first + 3, k_n)):
                    hit = jnp.where(ws[k] == at, us[k], 0)
                    acc = hit if acc is None else acc + hit
                even.append(acc & low)
                odd.append((acc >> 2) & low)
            halves[0].append(functools.reduce(lambda p, q: p + q, even))
            halves[1].append(functools.reduce(lambda p, q: p + q, odd))
        for parity in range(2):
            for t in range(0, WB // 8, 2):
                words = jnp.concatenate(halves[parity][t : t + 2], 0)
                for b in range(8):
                    if b < 7:
                        field = words & (15 << (4 * b))
                    else:
                        field = lax.shift_right_logical(words, jnp.full_like(words, 28))
                    at = (2 * b + parity) * WB + t * 8
                    c_ref[at : at + 16, cols] = field.astype(jnp.float32).astype(jnp.bfloat16)


def field_scale(b):
    return 2.0 ** (-4 * b) if b < 7 else 1.0


class Place:
    def __init__(self):
        clique, copy = lax.axis_index("clique"), lax.axis_index("copy")
        self.x, self.y = clique % 4, (clique // 4) * 2 + (copy // 2) % 2
        self.z, self.core = copy // 4, copy % 2
        self.member = self.x * 4 + self.y

    def device(self, x, y, z, core):
        return ((y // 2) * 4 + x, z * 4 + (y % 2) * 2 + core)

    def mate(self):
        return self.device(self.x, self.y, self.z, 1 - self.core)

    def plane(self):
        for dx in range(4):
            for dy in range(4):
                if dx or dy:
                    x, y = (self.x + dx) % 4, (self.y + dy) % 4
                    yield x * 4 + y, self.device(x, y, self.z, self.core)

    def column(self, steps):
        for dz in steps:
            z = (self.z + dz) % 8
            yield z, self.device(self.x, self.y, z, self.core)


def remote(src, dst, send, recv, device):
    return pltpu.make_async_remote_copy(
        src_ref=src, dst_ref=dst, send_sem=send, recv_sem=recv, device_id=device, device_id_type=MESH
    )


class Gather:
    def __init__(self, here, own, feats, send, recv):
        h, q, e = BLK // 2, BLK // 4, BLK // 8
        self.out, self.into = [], []
        right = here.device((here.x + 1) % 4, here.y, here.z, here.core)
        left = here.device((here.x + 3) % 4, here.y, here.z, here.core)
        across = here.device(here.x, 3 - here.y, here.z, here.core)
        up = here.device(here.x, here.y, (here.z + 1) % 8, here.core)
        down = here.device(here.x, here.y, (here.z + 7) % 8, here.core)
        mate = here.mate()
        hi = here.y // 2
        p = (here.z % 2) * q
        o = q - p

        def rows(piece, core):
            dx, flip, start, count = piece
            block = (1 - hi if flip else hi) * 4 + (here.x + dx) % 4
            return feats.at[pl.ds(pl.multiple_of(block * BLK + core * h + start, 16), count), :]

        def add(to, piece, got, source=None):
            i = len(self.out)
            dst = rows(piece, here.core)
            self.out.append(remote(dst if source is None else source, dst, send.at[i], recv.at[i], to))
            land = rows(got, 1 - here.core if to is mate else here.core)
            self.into.append(remote(land, land, send.at[i], recv.at[i], to))

        mine = own.at[pl.ds(pl.multiple_of(here.core * h + p, e), q), :]
        N, F = False, True
        add(right, (0, N, p, q), (3, N, p, q), mine)
        add(left, (0, N, p, q), (1, N, p, q), mine)
        add(across, (0, N, p, q), (0, F, p, q), mine)
        add(right, (3, N, p, e), (2, N, p, e))
        add(left, (1, N, p + e, e), (2, N, p + e, e))
        add(right, (0, F, p, q), (3, F, p, q))
        add(left, (0, F, p, q), (1, F, p, q))
        add(up, (3, N, p, q), (3, N, o, q))
        add(down, (1, N, p, q), (1, N, o, q))
        add(up, (0, F, p, q), (0, F, o, q))
        for piece in ((3, N, p, q), (1, N, p, q), (0, F, p, q)):
            add(mate, piece, piece)
        add(across, (2, N, p + 80, 48), (2, F, p + 80, 48))
        add(down, (2, N, p, q), (2, N, o, q))
        add(up, (3, F, p, q), (3, F, o, q))
        add(down, (1, F, p, q), (1, F, o, q))
        for piece in ((2, N, p, q), (3, F, p, q), (1, F, p, q)):
            add(mate, piece, piece)
        add(up, (2, F, p, e), (2, F, o, e))
        add(down, (2, F, p + e, e), (2, F, o + e, e))
        add(mate, (2, F, p, q), (2, F, p, q))
        for piece in ((3, N, o, q), (1, N, o, q), (0, F, o, q)):
            add(mate, piece, piece)
        for piece in ((2, N, o, q), (3, F, o, q), (1, F, o, q), (2, F, o, q)):
            add(mate, piece, piece)
        add(right, (3, F, p, 48), (2, F, p, 48))
        add(left, (1, F, p + 48, 32), (2, F, p + 48, 32))

    def run(self, *steps):
        for got, go in steps:
            for i in got:
                self.into[i].wait_recv()
            for i in go:
                self.out[i].start()

    def first(self):
        self.run(((), (0, 1, 2)))

    def second(self):
        self.run(((0,), (3,)), ((1,), (4,)), ((2,), (5, 6, 9, 7, 8)), ((), (10, 11, 12)))

    def third(self):
        self.run(((3, 4), (13, 14, 17)))

    def third_across(self):
        self.run(((5,), (30, 15)), ((6,), (31, 16)), ((), (18, 19)), ((7,), (23,)), ((8,), (24,)), ((9,), (25,)))

    def fourth(self):
        self.run(((13, 30, 31), (20, 21, 22)))

    def fifth(self):
        self.run(((14,), (26,)), ((15,), (27,)), ((16,), (28,)), ((20, 21), (29,)))

    def sixth(self):
        self.run(((10, 11, 12, 17, 18, 19, *range(22, 30)), ()))

    def finish(self):
        for c in self.out:
            c.wait_send()


class Sum:
    def __init__(self, here, bufs, sems):
        self.here = here
        self.g, self.rc, self.hs, self.ra, self.ms, self.rb, self.out = bufs
        c_s, c_r, a_s, a_r, b_s, b_r, e_s, e_r, f_s, f_r = sems
        g, rc, hs, ra, ms, rb, out = bufs
        half = rc.shape[0]
        per = half // 16
        mate, me = here.mate(), here.member
        plane = list(here.plane())
        column = list(here.column(range(1, 8)))
        self.mine, self.other = here.core * half, (1 - here.core) * half
        self.half, self.per = half, per
        self.swap = remote(g.at[pl.ds(self.other, half)], rc, c_s, c_r, mate)
        self.to_plane = [
            remote(hs.at[pl.ds(q * per, per)], ra.at[me], a_s.at[q], a_r.at[me], d) for q, d in plane
        ]
        self.of_plane = [
            remote(hs.at[pl.ds(q * per, per)], ra.at[q], a_s.at[q], a_r.at[q], d) for q, d in plane
        ]

        self.to_column = [remote(ms, rb.at[here.z], b_s.at[z], b_r.at[here.z], d) for z, d in column]
        self.of_column = [remote(ms, rb.at[z], b_s.at[z], b_r.at[z], d) for z, d in column]
        self.slot = slot = pl.ds(self.mine + me * per, per)
        self.home_to, self.home_of, self.pass_to, self.pass_of = [], [], [], []
        for q, d in plane:
            at = out.at[pl.ds(self.mine + q * per, per)]
            self.home_to.append(remote(out.at[slot], out.at[slot], e_s.at[q], e_r.at[me], d))
            self.home_of.append(remote(at, at, e_s.at[q], e_r.at[q], d))
            self.pass_to.append(remote(at, at, f_s.at[q], f_r.at[q], mate))
        self.own_to = remote(out.at[slot], out.at[slot], f_s.at[me], f_r.at[me], mate)
        for q in range(16):
            at = out.at[pl.ds(self.other + q * per, per)]
            self.pass_of.append(remote(at, at, f_s.at[q], f_r.at[q], mate))

    def to_pair(self):
        self.swap.start()

    def to_the_plane(self):
        f32 = jnp.float32
        self.swap.wait_recv()
        both = self.g[pl.ds(self.mine, self.half)].astype(f32) + self.rc[...].astype(f32)
        self.hs[...] = both.astype(jnp.bfloat16)
        for c in self.to_plane:
            c.start()
        self.ra[self.here.member] = self.hs[pl.ds(self.here.member * self.per, self.per)]

    def to_the_column(self):
        for c in self.of_plane:
            c.wait_recv()
        self.ms[...] = jnp.sum(self.ra[...].astype(jnp.float32), axis=0).astype(jnp.bfloat16)
        for c in self.to_column:
            c.start()
        self.rb[self.here.z] = self.ms[...]

    def back_in_plane(self):
        for c in self.of_column:
            c.wait_recv()
        self.out[self.slot] = jnp.sum(self.rb[...].astype(jnp.float32), axis=0).astype(jnp.bfloat16)
        for c in self.home_to:
            c.start()
        self.own_to.start()

    def back_to_pair(self):
        for c, then in zip(self.home_of, self.pass_to):
            c.wait_recv()
            then.start()

    def received(self):
        for c in self.pass_of:
            c.wait_recv()

    def finish(self):
        sent = [self.swap, *self.to_plane, *self.to_column, *self.home_to, *self.pass_to]
        for c in [*sent, self.own_to]:
            c.wait_send()


def whole_kernel(
    fanout, cnt_ref, og_hbm, pa_hbm, l2_hbm, hs_hbm, ci_hbm, hf_hbm, cf_hbm, one_ref, two_ref,
    og, pa, l2, hs, ci, hu, cu, feats, rg, hp, c0, c1, acc, sems, g_send, g_recv, one_bufs, one_sems, two_bufs, two_sems,
):
    rows, dh = og.shape
    din = feats.shape[1]
    tile = 512
    hot_n = hf_hbm.shape[0] * 8
    here = Place()
    gather = Gather(here, hf_hbm, feats, g_send, g_recv)
    sums_one = [Sum(here, b, m) for b, m in zip(one_bufs, one_sems)]
    sum_two = Sum(here, two_bufs, two_sems)
    home = pl.ds(pl.multiple_of(lax.axis_index("clique") * BLK, BLK), BLK)
    pairs = [
        (l2_hbm, l2),
        (og_hbm, og),
        (pa_hbm, pa),
        (ci_hbm, ci),
        (hs_hbm, hs),
        (cf_hbm, feats.at[pl.ds(hot_n, cf_hbm.shape[0]), :]),
        (hf_hbm, feats.at[home, :]),
    ]
    copies = [pltpu.make_async_copy(s, d, sems.at[i]) for i, (s, d) in enumerate(pairs)]
    barrier = pltpu.get_barrier_semaphore()
    peers = [here.mate()] + [d for _, d in here.plane()] + [d for _, d in here.column(range(1, 8))]
    for d in peers:
        pl.semaphore_signal(barrier, inc=1, device_id=d, device_id_type=MESH)
    for c in copies:
        c.start()
    pl.semaphore_wait(barrier, len(peers))
    gather.first()
    for c in copies[:3]:
        c.wait()
    count = cnt_ref[0]
    acc[:dh, :] = jnp.zeros((dh, dh), jnp.float32)

    def some_rows(i, carry):
        at = pl.ds(pl.multiple_of(i * tile, tile), tile)
        live = (lax.broadcasted_iota(jnp.int32, (tile, 1), 0) + i * tile) < count
        o = og[at, :]
        masked = jnp.where(live, o, jnp.zeros_like(o))
        p = pa[at, :]
        back = lax.dot_general(
            masked, l2[...], (((1,), (1,)), ((), ())), preferred_element_type=jnp.float32
        )
        rg[at, :] = jnp.where(p > 0, back, 0.0).astype(jnp.bfloat16)
        activ = jnp.maximum(p, jnp.zeros_like(p))
        acc[:dh, :] += lax.dot_general(
            activ, masked, (((0,), (0,)), ((), ())), preferred_element_type=jnp.float32
        )
        return carry

    lax.fori_loop(0, rows // tile, some_rows, 0)
    sum_two.g[...] = acc[:dh, :].reshape(dh // 8, 8, dh).astype(jnp.bfloat16)
    sum_two.to_pair()
    for c in copies[3:5]:
        c.wait()
    split_indices(ci, cu)
    split_indices(hs, hu)
    n_hot = hot_n // BLK

    def step(refs, block, c_new, c_old, base):
        if refs is not None:
            build_counts(*refs, block, c_new)
        p = jnp.dot(c_old[...], rg[...], preferred_element_type=jnp.float32)
        size = BLK // 8
        for b in range(8):
            at = pl.ds(pl.multiple_of(base + b * size, size), size)
            scaled = p[b * size : b * size + size] * (field_scale(b) / fanout)
            hp[at, :] = scaled.astype(jnp.bfloat16)

    cold, warm = (ci, cu), (hs, hu)
    build_counts(*cold, 0, c0)
    step(cold, 1, c1, c0, hot_n)
    gather.second()
    step(cold, 2, c0, c1, hot_n + BLK)
    step(cold, 3, c1, c0, hot_n + 2 * BLK)
    step(warm, 0, c0, c1, hot_n + 3 * BLK)

    def hot(i, carry):
        step(warm, 2 * i + 1, c1, c0, 2 * i * BLK)
        step(warm, 2 * i + 2, c0, c1, (2 * i + 1) * BLK)

        @pl.when(i == 0)
        def _():
            gather.third()

        @pl.when(i == 1)
        def _():
            gather.third_across()

        return carry

    lax.fori_loop(0, n_hot // 2 - 1, hot, 0)
    step(warm, n_hot - 1, c1, c0, (n_hot - 2) * BLK)
    gather.fourth()
    sum_two.to_the_plane()
    step(None, 0, c0, c1, (n_hot - 1) * BLK)
    for c in copies[5:]:
        c.wait()
    turned = (((0,), (0,)), ((), ()))
    acc[...] = lax.dot_general(
        feats[hot_n:, :], hp[hot_n:, :], turned, preferred_element_type=jnp.float32
    )
    gather.fifth()
    gather.sixth()
    width = din // len(sums_one)

    def some_sums(n):
        at = slice(n * width, n * width + width)
        sums = acc[at, :] + lax.dot_general(
            feats[:hot_n, at], hp[:hot_n, :], turned, preferred_element_type=jnp.float32
        )
        sums_one[n].g[...] = sums.reshape(width // 8, 8, dh).astype(jnp.bfloat16)
        sums_one[n].to_pair()

    some_sums(0)
    some_sums(1)
    sums_one[0].to_the_plane()
    sum_two.to_the_column()
    some_sums(2)
    sums_one[1].to_the_plane()
    sums_one[2].to_the_plane()
    for one in sums_one:
        one.to_the_column()
    sum_two.back_in_plane()
    for one in sums_one:
        one.back_in_plane()
    sum_two.back_to_pair()
    for one in sums_one:
        one.back_to_pair()
    sum_two.received()
    two_ref[...] = sum_two.out[...]
    for n, one in enumerate(sums_one):
        one.received()
        one_ref[n * width // 8 : (n + 1) * width // 8] = one.out[...]
    gather.finish()
    sum_two.finish()
    for one in sums_one:
        one.finish()


def sum_scratch(rows, dh):
    vm, dma, bf16 = pltpu.VMEM, pltpu.SemaphoreType.DMA, jnp.bfloat16
    units = rows // 8
    half, per = units // 2, units // 32
    bufs = (
        vm((units, 8, dh), bf16),
        vm((half, 8, dh), bf16),
        vm((half, 8, dh), bf16),
        vm((16, per, 8, dh), bf16),
        vm((per, 8, dh), bf16),
        vm((8, per, 8, dh), bf16),
        vm((units, 8, dh), bf16),
    )
    sems = [dma, dma] + [dma((n,)) for n in (16, 16, 8, 8, 16, 16, 16, 16)]
    return bufs, tuple(sems)


def whole_call(fanout, og, pa, cnt, l2, hs, ci, hf, cf):
    vm, dma = pltpu.VMEM, pltpu.SemaphoreType.DMA
    hbm = pl.BlockSpec(memory_space=pltpu.HBM)
    bf16 = jnp.bfloat16
    rows, dh = og.shape
    din = hf.shape[1]
    slots = hf.shape[0] * 8 + cf.shape[0]
    chunks = [sum_scratch(din // 3, dh) for _ in range(3)]
    one_bufs, one_sems = tuple(c[0] for c in chunks), tuple(c[1] for c in chunks)
    two_bufs, two_sems = sum_scratch(dh, dh)
    return pl.pallas_call(
        functools.partial(whole_kernel, fanout),
        out_shape=(
            jax.ShapeDtypeStruct((din // 8, 8, dh), bf16),
            jax.ShapeDtypeStruct((dh // 8, 8, dh), bf16),
        ),
        in_specs=[pl.BlockSpec(memory_space=pltpu.SMEM)] + [hbm] * 7,
        out_specs=[pl.BlockSpec(memory_space=vm)] * 2,
        scratch_shapes=[
            vm((rows, dh), bf16),
            vm((rows, dh), bf16),
            vm((dh, dh), bf16),
            vm((hs.shape[1], rows), jnp.int32),
            vm((ci.shape[1], rows), jnp.int32),
            vm((hs.shape[1], rows), jnp.int32),
            vm((ci.shape[1], rows), jnp.int32),
            vm((slots, din), bf16),
            vm((rows, dh), bf16),
            vm((slots, dh), bf16),
            vm((BLK, rows), bf16),
            vm((BLK, rows), bf16),
            vm((din, dh), jnp.float32),
            dma((7,)),
            dma((32,)),
            dma((32,)),
            one_bufs,
            one_sems,
            two_bufs,
            two_sems,
        ],
        compiler_params=pltpu.CompilerParams(
            collective_id=0, has_side_effects=True, vmem_limit_bytes=58 << 20
        ),
    )(cnt, og, pa, l2, hs.T, ci.T, hf, cf)


def on_device(
    out_grad, pre_act, batch_count, layer_two, hot_slots, cold_index, hot_feats, cold_feats
):
    fanout = hot_slots.shape[1] + cold_index.shape[1]
    one, two = whole_call(
        fanout, out_grad, pre_act, batch_count, layer_two, hot_slots, cold_index, hot_feats, cold_feats
    )
    dh = out_grad.shape[1]
    return one.reshape(-1, dh).astype(jnp.float32), two.reshape(-1, dh).astype(jnp.float32)


def solution(mesh):
    placed = (
        P(("clique", "copy"), None),
        P(("clique", "copy"), None),
        P(("clique", "copy")),
        P(),
        P(("clique", "copy"), None),
        P(("clique", "copy"), None),
        P("clique", None),
        P(("clique", "copy"), None),
    )
    return jax.shard_map(
        on_device, mesh=mesh, in_specs=placed, out_specs=(P(), P()), check_vma=False
    )
```

```python
import functools
import jax
import jax.numpy as jnp
from jax import lax
from jax.experimental import pallas as pl
from jax.experimental.pallas import tpu as pltpu
from jax.sharding import PartitionSpec as P

MESH = pl.DeviceIdType.MESH
BLK = 512
FIELDS = 16
WB = BLK // FIELDS
LANES = 128


def split_indices(idx_ref, unit_ref):
    idx = idx_ref[...]
    unit_ref[...] = jnp.left_shift(jnp.ones_like(idx), ((idx >> 5) & 15) * 2)
    idx_ref[...] = (idx >> 9) * WB + (idx & (WB - 1))


def build_counts(word_ref, unit_ref, block, c_ref, share=(0, 1)):
    k_n, rows = word_ref.shape
    assert k_n <= 15
    sub = lax.broadcasted_iota(jnp.int32, (8, LANES), 0) + block * WB
    low = jnp.full((8, LANES), 0x33333333, jnp.int32)
    part = rows // LANES // share[1]
    for j in range(share[0] * part, share[0] * part + part):
        cols = slice(j * LANES, j * LANES + LANES)
        ws = [jnp.broadcast_to(word_ref[k : k + 1, cols], (8, LANES)) for k in range(k_n)]
        us = [jnp.broadcast_to(unit_ref[k : k + 1, cols], (8, LANES)) for k in range(k_n)]
        halves = ([], [])
        for t in range(WB // 8):
            at = sub + t * 8
            even, odd = [], []
            for first in range(0, k_n, 3):
                acc = None
                for k in range(first, min(first + 3, k_n)):
                    hit = jnp.where(ws[k] == at, us[k], 0)
                    acc = hit if acc is None else acc + hit
                even.append(acc & low)
                odd.append((acc >> 2) & low)
            halves[0].append(functools.reduce(lambda p, q: p + q, even))
            halves[1].append(functools.reduce(lambda p, q: p + q, odd))
        for parity in range(2):
            for t in range(0, WB // 8, 2):
                words = jnp.concatenate(halves[parity][t : t + 2], 0)
                for b in range(8):
                    if b < 7:
                        field = words & (15 << (4 * b))
                    else:
                        field = lax.shift_right_logical(words, jnp.full_like(words, 28))
                    at = (2 * b + parity) * WB + t * 8
                    c_ref[at : at + 16, cols] = field.astype(jnp.float32).astype(jnp.bfloat16)


def field_scale(b):
    return 2.0 ** (-4 * b) if b < 7 else 1.0


class Place:
    def __init__(self):
        clique, copy = lax.axis_index("clique"), lax.axis_index("copy")
        self.x, self.y = clique % 4, (clique // 4) * 2 + (copy // 2) % 2
        self.z, self.core = copy // 4, copy % 2
        self.member = self.x * 4 + self.y

    def device(self, x, y, z, core):
        return ((y // 2) * 4 + x, z * 4 + (y % 2) * 2 + core)

    def mate(self):
        return self.device(self.x, self.y, self.z, 1 - self.core)

    def plane(self):
        for dx in range(4):
            for dy in range(4):
                if dx or dy:
                    x, y = (self.x + dx) % 4, (self.y + dy) % 4
                    yield x * 4 + y, self.device(x, y, self.z, self.core)

    def column(self, steps):
        for dz in steps:
            z = (self.z + dz) % 8
            yield z, self.device(self.x, self.y, z, self.core)


def remote(src, dst, send, recv, device):
    return pltpu.make_async_remote_copy(
        src_ref=src, dst_ref=dst, send_sem=send, recv_sem=recv, device_id=device, device_id_type=MESH
    )


class Gather:
    def __init__(self, here, own, feats, send, recv):
        h, q, e = BLK // 2, BLK // 4, BLK // 8
        self.out, self.into = [], []
        right = here.device((here.x + 1) % 4, here.y, here.z, here.core)
        left = here.device((here.x + 3) % 4, here.y, here.z, here.core)
        across = here.device(here.x, 3 - here.y, here.z, here.core)
        up = here.device(here.x, here.y, (here.z + 1) % 8, here.core)
        down = here.device(here.x, here.y, (here.z + 7) % 8, here.core)
        mate = here.mate()
        hi = here.y // 2
        p = (here.z % 2) * q
        o = q - p

        def rows(piece, core):
            dx, flip, start, count = piece
            block = (1 - hi if flip else hi) * 4 + (here.x + dx) % 4
            return feats.at[pl.ds(pl.multiple_of(block * BLK + core * h + start, 16), count), :]

        def add(to, piece, got, source=None):
            i = len(self.out)
            dst = rows(piece, here.core)
            self.out.append(remote(dst if source is None else source, dst, send.at[i], recv.at[i], to))
            land = rows(got, 1 - here.core if to is mate else here.core)
            self.into.append(remote(land, land, send.at[i], recv.at[i], to))

        mine = own.at[pl.ds(pl.multiple_of(here.core * h + p, e), q), :]
        N, F = False, True
        add(right, (0, N, p, q), (3, N, p, q), mine)
        add(left, (0, N, p, q), (1, N, p, q), mine)
        add(across, (0, N, p, q), (0, F, p, q), mine)
        add(right, (3, N, p, e), (2, N, p, e))
        add(left, (1, N, p + e, e), (2, N, p + e, e))
        add(right, (0, F, p, q), (3, F, p, q))
        add(left, (0, F, p, q), (1, F, p, q))
        add(up, (3, N, p, q), (3, N, o, q))
        add(down, (1, N, p, q), (1, N, o, q))
        add(up, (0, F, p, q), (0, F, o, q))
        for piece in ((3, N, p, q), (1, N, p, q), (0, F, p, q)):
            add(mate, piece, piece)
        add(across, (2, N, p + 80, 48), (2, F, p + 80, 48))
        add(down, (2, N, p, q), (2, N, o, q))
        add(up, (3, F, p, q), (3, F, o, q))
        add(down, (1, F, p, q), (1, F, o, q))
        for piece in ((2, N, p, q), (3, F, p, q), (1, F, p, q)):
            add(mate, piece, piece)
        add(up, (2, F, p, e), (2, F, o, e))
        add(down, (2, F, p + e, e), (2, F, o + e, e))
        add(mate, (2, F, p, q), (2, F, p, q))
        for piece in ((3, N, o, q), (1, N, o, q), (0, F, o, q)):
            add(mate, piece, piece)
        for piece in ((2, N, o, q), (3, F, o, q), (1, F, o, q), (2, F, o, q)):
            add(mate, piece, piece)
        add(right, (3, F, p, 48), (2, F, p, 48))
        add(left, (1, F, p + 48, 32), (2, F, p + 48, 32))

    def run(self, *steps):
        for got, go in steps:
            for i in got:
                self.into[i].wait_recv()
            for i in go:
                self.out[i].start()

    def first(self):
        self.run(((), (0, 1, 2)))

    def second(self):
        self.run(((0,), (3,)), ((1,), (4,)), ((2,), (5, 6, 9, 7, 8)), ((), (10, 11, 12)))

    def third(self):
        self.run(((3, 4), (13, 14, 17)))

    def third_across(self):
        self.run(((5,), (30, 15)), ((6,), (31, 16)), ((), (18, 19)), ((7,), (23,)), ((8,), (24,)), ((9,), (25,)))

    def fourth(self):
        self.run(((13, 30, 31), (20, 21, 22)))

    def fifth(self):
        self.run(((14,), (26,)), ((15,), (27,)), ((16,), (28,)), ((20, 21), (29,)))

    def sixth(self):
        self.run(((10, 11, 12, 17, 18, 19, *range(22, 30)), ()))

    def finish(self):
        for c in self.out:
            c.wait_send()


class Sum:
    def __init__(self, here, bufs, sems):
        self.here = here
        self.g, self.rc, self.hs, self.ra, self.ms, self.rb, self.out = bufs
        c_s, c_r, a_s, a_r, b_s, b_r, e_s, e_r, f_s, f_r = sems
        g, rc, hs, ra, ms, rb, out = bufs
        half = rc.shape[0]
        per = half // 16
        mate, me = here.mate(), here.member
        plane = list(here.plane())
        column = list(here.column(range(1, 8)))
        self.mine, self.other = here.core * half, (1 - here.core) * half
        self.half, self.per = half, per
        self.swap = remote(g.at[pl.ds(self.other, half)], rc, c_s, c_r, mate)
        self.to_plane = [
            remote(hs.at[pl.ds(q * per, per)], ra.at[me], a_s.at[q], a_r.at[me], d) for q, d in plane
        ]
        self.of_plane = [
            remote(hs.at[pl.ds(q * per, per)], ra.at[q], a_s.at[q], a_r.at[q], d) for q, d in plane
        ]

        self.to_column = [remote(ms, rb.at[here.z], b_s.at[z], b_r.at[here.z], d) for z, d in column]
        self.of_column = [remote(ms, rb.at[z], b_s.at[z], b_r.at[z], d) for z, d in column]
        self.slot = slot = pl.ds(self.mine + me * per, per)
        self.home_to, self.home_of, self.pass_to, self.pass_of = [], [], [], []
        for q, d in plane:
            at = out.at[pl.ds(self.mine + q * per, per)]
            self.home_to.append(remote(out.at[slot], out.at[slot], e_s.at[q], e_r.at[me], d))
            self.home_of.append(remote(at, at, e_s.at[q], e_r.at[q], d))
            self.pass_to.append(remote(at, at, f_s.at[q], f_r.at[q], mate))
        self.own_to = remote(out.at[slot], out.at[slot], f_s.at[me], f_r.at[me], mate)
        for q in range(16):
            at = out.at[pl.ds(self.other + q * per, per)]
            self.pass_of.append(remote(at, at, f_s.at[q], f_r.at[q], mate))

    def to_pair(self):
        self.swap.start()

    def to_the_plane(self):
        f32 = jnp.float32
        self.swap.wait_recv()
        both = self.g[pl.ds(self.mine, self.half)].astype(f32) + self.rc[...].astype(f32)
        self.hs[...] = both.astype(jnp.bfloat16)
        for c in self.to_plane:
            c.start()
        self.ra[self.here.member] = self.hs[pl.ds(self.here.member * self.per, self.per)]

    def to_the_column(self):
        for c in self.of_plane:
            c.wait_recv()
        self.ms[...] = jnp.sum(self.ra[...].astype(jnp.float32), axis=0).astype(jnp.bfloat16)
        for c in self.to_column:
            c.start()
        self.rb[self.here.z] = self.ms[...]

    def back_in_plane(self):
        for c in self.of_column:
            c.wait_recv()
        self.out[self.slot] = jnp.sum(self.rb[...].astype(jnp.float32), axis=0).astype(jnp.bfloat16)
        for c in self.home_to:
            c.start()
        self.own_to.start()

    def back_to_pair(self):
        for c, then in zip(self.home_of, self.pass_to):
            c.wait_recv()
            then.start()

    def received(self):
        for c in self.pass_of:
            c.wait_recv()

    def finish(self):
        sent = [self.swap, *self.to_plane, *self.to_column, *self.home_to, *self.pass_to]
        for c in [*sent, self.own_to]:
            c.wait_send()


def whole_kernel(
    fanout, cnt_ref, og_hbm, pa_hbm, l2_hbm, hs_hbm, ci_hbm, hf_hbm, cf_hbm, one_ref, two_ref,
    og, pa, l2, hs, ci, hu, cu, feats, rg, hp, c0, c1, acc, sems, tile_sems, g_send, g_recv, one_bufs, one_sems, two_bufs, two_sems,
):
    rows, dh = og.shape
    din = feats.shape[1]
    tile = 512
    hot_n = hf_hbm.shape[0] * 8
    here = Place()
    gather = Gather(here, hf_hbm, feats, g_send, g_recv)
    sums_one = [Sum(here, b, m) for b, m in zip(one_bufs, one_sems)]
    sum_two = Sum(here, two_bufs, two_sems)
    home = pl.ds(pl.multiple_of(lax.axis_index("clique") * BLK, BLK), BLK)
    pairs = [
        (l2_hbm, l2),
        (ci_hbm, ci),
        (hs_hbm, hs),
        (cf_hbm, feats.at[pl.ds(hot_n, cf_hbm.shape[0]), :]),
        (hf_hbm, feats.at[home, :]),
    ]
    copies = [pltpu.make_async_copy(s, d, sems.at[i]) for i, (s, d) in enumerate(pairs)]
    tiles = []
    for i in range(rows // tile):
        at = pl.ds(i * tile, tile)
        for n, (s, d) in enumerate(((og_hbm, og), (pa_hbm, pa))):
            tiles.append(pltpu.make_async_copy(s.at[at, :], d.at[at, :], tile_sems.at[2 * i + n]))
    barrier = pltpu.get_barrier_semaphore()
    peers = [here.mate()] + [d for _, d in here.plane()] + [d for _, d in here.column(range(1, 8))]
    for d in peers:
        pl.semaphore_signal(barrier, inc=1, device_id=d, device_id_type=MESH)
    for c in [copies[1], copies[0], *tiles, *copies[2:]]:
        c.start()
    pl.semaphore_wait(barrier, len(peers))
    gather.first()
    count = cnt_ref[0]
    acc[:dh, :] = jnp.zeros((dh, dh), jnp.float32)
    copies[1].wait()
    split_indices(ci, cu)
    copies[0].wait()
    for i in range(rows // tile):
        tiles[2 * i].wait()
        tiles[2 * i + 1].wait()
        at = slice(i * tile, i * tile + tile)
        live = (lax.broadcasted_iota(jnp.int32, (tile, 1), 0) + i * tile) < count
        o = og[at, :]
        masked = jnp.where(live, o, jnp.zeros_like(o))
        p = pa[at, :]
        back = lax.dot_general(
            masked, l2[...], (((1,), (1,)), ((), ())), preferred_element_type=jnp.float32
        )
        rg[at, :] = jnp.where(p > 0, back, 0.0).astype(jnp.bfloat16)
        activ = jnp.maximum(p, jnp.zeros_like(p))
        acc[:dh, :] += lax.dot_general(
            activ, masked, (((0,), (0,)), ((), ())), preferred_element_type=jnp.float32
        )
        build_counts(ci, cu, 0, c0, (i, rows // tile))
    sum_two.g[...] = acc[:dh, :].reshape(dh // 8, 8, dh).astype(jnp.bfloat16)
    sum_two.to_pair()
    copies[2].wait()
    split_indices(hs, hu)
    n_hot = hot_n // BLK

    def step(refs, block, c_new, c_old, base):
        if refs is not None:
            build_counts(*refs, block, c_new)
        p = jnp.dot(c_old[...], rg[...], preferred_element_type=jnp.float32)
        size = BLK // 8
        for b in range(8):
            at = pl.ds(pl.multiple_of(base + b * size, size), size)
            scaled = p[b * size : b * size + size] * (field_scale(b) / fanout)
            hp[at, :] = scaled.astype(jnp.bfloat16)

    cold, warm = (ci, cu), (hs, hu)
    step(cold, 1, c1, c0, hot_n)
    gather.second()
    step(cold, 2, c0, c1, hot_n + BLK)
    step(cold, 3, c1, c0, hot_n + 2 * BLK)
    step(warm, 0, c0, c1, hot_n + 3 * BLK)

    def hot(i, carry):
        step(warm, 2 * i + 1, c1, c0, 2 * i * BLK)
        step(warm, 2 * i + 2, c0, c1, (2 * i + 1) * BLK)

        @pl.when(i == 0)
        def _():
            gather.third()

        @pl.when(i == 1)
        def _():
            gather.third_across()

        return carry

    lax.fori_loop(0, n_hot // 2 - 1, hot, 0)
    step(warm, n_hot - 1, c1, c0, (n_hot - 2) * BLK)
    gather.fourth()
    sum_two.to_the_plane()
    step(None, 0, c0, c1, (n_hot - 1) * BLK)
    for c in copies[3:]:
        c.wait()
    turned = (((0,), (0,)), ((), ()))
    acc[...] = lax.dot_general(
        feats[hot_n:, :], hp[hot_n:, :], turned, preferred_element_type=jnp.float32
    )
    gather.fifth()
    gather.sixth()
    sum_two.to_the_column()
    width = din // len(sums_one)

    def some_sums(n):
        at = slice(n * width, n * width + width)
        sums = acc[at, :] + lax.dot_general(
            feats[:hot_n, at], hp[:hot_n, :], turned, preferred_element_type=jnp.float32
        )
        sums_one[n].g[...] = sums.reshape(width // 8, 8, dh).astype(jnp.bfloat16)
        sums_one[n].to_pair()

    some_sums(0)
    some_sums(1)
    sums_one[0].to_the_plane()
    some_sums(2)
    sums_one[1].to_the_plane()
    sums_one[2].to_the_plane()
    sum_two.back_in_plane()
    for one in sums_one:
        one.to_the_column()
    for one in sums_one:
        one.back_in_plane()
    sum_two.back_to_pair()
    for one in sums_one:
        one.back_to_pair()
    sum_two.received()
    two_ref[...] = sum_two.out[...]
    for n, one in enumerate(sums_one):
        one.received()
        one_ref[n * width // 8 : (n + 1) * width // 8] = one.out[...]
    gather.finish()
    sum_two.finish()
    for one in sums_one:
        one.finish()


def sum_scratch(rows, dh):
    vm, dma, bf16 = pltpu.VMEM, pltpu.SemaphoreType.DMA, jnp.bfloat16
    units = rows // 8
    half, per = units // 2, units // 32
    bufs = (
        vm((units, 8, dh), bf16),
        vm((half, 8, dh), bf16),
        vm((half, 8, dh), bf16),
        vm((16, per, 8, dh), bf16),
        vm((per, 8, dh), bf16),
        vm((8, per, 8, dh), bf16),
        vm((units, 8, dh), bf16),
    )
    sems = [dma, dma] + [dma((n,)) for n in (16, 16, 8, 8, 16, 16, 16, 16)]
    return bufs, tuple(sems)


def whole_call(fanout, og, pa, cnt, l2, hs, ci, hf, cf):
    vm, dma = pltpu.VMEM, pltpu.SemaphoreType.DMA
    hbm = pl.BlockSpec(memory_space=pltpu.HBM)
    bf16 = jnp.bfloat16
    rows, dh = og.shape
    din = hf.shape[1]
    slots = hf.shape[0] * 8 + cf.shape[0]
    chunks = [sum_scratch(din // 3, dh) for _ in range(3)]
    one_bufs, one_sems = tuple(c[0] for c in chunks), tuple(c[1] for c in chunks)
    two_bufs, two_sems = sum_scratch(dh, dh)
    return pl.pallas_call(
        functools.partial(whole_kernel, fanout),
        out_shape=(
            jax.ShapeDtypeStruct((din // 8, 8, dh), bf16),
            jax.ShapeDtypeStruct((dh // 8, 8, dh), bf16),
        ),
        in_specs=[pl.BlockSpec(memory_space=pltpu.SMEM)] + [hbm] * 7,
        out_specs=[pl.BlockSpec(memory_space=vm)] * 2,
        scratch_shapes=[
            vm((rows, dh), bf16),
            vm((rows, dh), bf16),
            vm((dh, dh), bf16),
            vm((hs.shape[1], rows), jnp.int32),
            vm((ci.shape[1], rows), jnp.int32),
            vm((hs.shape[1], rows), jnp.int32),
            vm((ci.shape[1], rows), jnp.int32),
            vm((slots, din), bf16),
            vm((rows, dh), bf16),
            vm((slots, dh), bf16),
            vm((BLK, rows), bf16),
            vm((BLK, rows), bf16),
            vm((din, dh), jnp.float32),
            dma((5,)),
            dma((2 * (rows // 512),)),
            dma((32,)),
            dma((32,)),
            one_bufs,
            one_sems,
            two_bufs,
            two_sems,
        ],
        compiler_params=pltpu.CompilerParams(
            collective_id=0, has_side_effects=True, vmem_limit_bytes=58 << 20
        ),
    )(cnt, og, pa, l2, hs.T, ci.T, hf, cf)


def on_device(
    out_grad, pre_act, batch_count, layer_two, hot_slots, cold_index, hot_feats, cold_feats
):
    fanout = hot_slots.shape[1] + cold_index.shape[1]
    one, two = whole_call(
        fanout, out_grad, pre_act, batch_count, layer_two, hot_slots, cold_index, hot_feats, cold_feats
    )
    dh = out_grad.shape[1]
    return one.reshape(-1, dh).astype(jnp.float32), two.reshape(-1, dh).astype(jnp.float32)


def solution(mesh):
    placed = (
        P(("clique", "copy"), None),
        P(("clique", "copy"), None),
        P(("clique", "copy")),
        P(),
        P(("clique", "copy"), None),
        P(("clique", "copy"), None),
        P("clique", None),
        P(("clique", "copy"), None),
    )
    return jax.shard_map(
        on_device, mesh=mesh, in_specs=placed, out_specs=(P(), P()), check_vma=False
    )
```

```python
import functools
import jax
import jax.numpy as jnp
from jax import lax
from jax.experimental import pallas as pl
from jax.experimental.pallas import tpu as pltpu
from jax.sharding import PartitionSpec as P

MESH = pl.DeviceIdType.MESH
BLK = 512
FIELDS = 16
WB = BLK // FIELDS
LANES = 128


def split_indices(idx_ref, unit_ref):
    idx = idx_ref[...]
    unit_ref[...] = jnp.left_shift(jnp.ones_like(idx), ((idx >> 5) & 15) * 2)
    idx_ref[...] = (idx >> 9) * WB + (idx & (WB - 1))


def build_counts(word_ref, unit_ref, block, c_ref, share=(0, 1)):
    k_n, rows = word_ref.shape
    assert k_n <= 15
    sub = lax.broadcasted_iota(jnp.int32, (8, LANES), 0) + block * WB
    low = jnp.full((8, LANES), 0x33333333, jnp.int32)
    part = rows // LANES // share[1]
    for j in range(share[0] * part, share[0] * part + part):
        cols = slice(j * LANES, j * LANES + LANES)
        ws = [jnp.broadcast_to(word_ref[k : k + 1, cols], (8, LANES)) for k in range(k_n)]
        us = [jnp.broadcast_to(unit_ref[k : k + 1, cols], (8, LANES)) for k in range(k_n)]
        halves = ([], [])
        for t in range(WB // 8):
            at = sub + t * 8
            even, odd = [], []
            for first in range(0, k_n, 3):
                acc = None
                for k in range(first, min(first + 3, k_n)):
                    hit = jnp.where(ws[k] == at, us[k], 0)
                    acc = hit if acc is None else acc + hit
                even.append(acc & low)
                odd.append((acc >> 2) & low)
            halves[0].append(functools.reduce(lambda p, q: p + q, even))
            halves[1].append(functools.reduce(lambda p, q: p + q, odd))
        for parity in range(2):
            for t in range(0, WB // 8, 2):
                words = jnp.concatenate(halves[parity][t : t + 2], 0)
                for b in range(8):
                    if b < 7:
                        field = words & (15 << (4 * b))
                    else:
                        field = lax.shift_right_logical(words, jnp.full_like(words, 28))
                    at = (2 * b + parity) * WB + t * 8
                    c_ref[at : at + 16, cols] = field.astype(jnp.float32).astype(jnp.bfloat16)


def field_scale(b):
    return 2.0 ** (-4 * b) if b < 7 else 1.0


class Place:
    def __init__(self):
        clique, copy = lax.axis_index("clique"), lax.axis_index("copy")
        self.x, self.y = clique % 4, (clique // 4) * 2 + (copy // 2) % 2
        self.z, self.core = copy // 4, copy % 2
        self.member = self.x * 4 + self.y

    def device(self, x, y, z, core):
        return ((y // 2) * 4 + x, z * 4 + (y % 2) * 2 + core)

    def mate(self):
        return self.device(self.x, self.y, self.z, 1 - self.core)

    def plane(self):
        for dx in range(4):
            for dy in range(4):
                if dx or dy:
                    x, y = (self.x + dx) % 4, (self.y + dy) % 4
                    yield x * 4 + y, self.device(x, y, self.z, self.core)

    def column(self, steps):
        for dz in steps:
            z = (self.z + dz) % 8
            yield z, self.device(self.x, self.y, z, self.core)


def remote(src, dst, send, recv, device):
    return pltpu.make_async_remote_copy(
        src_ref=src, dst_ref=dst, send_sem=send, recv_sem=recv, device_id=device, device_id_type=MESH
    )


class Gather:
    def __init__(self, here, own, feats, send, recv):
        h, q, e = BLK // 2, BLK // 4, BLK // 8
        self.out, self.into = [], []
        right = here.device((here.x + 1) % 4, here.y, here.z, here.core)
        left = here.device((here.x + 3) % 4, here.y, here.z, here.core)
        across = here.device(here.x, 3 - here.y, here.z, here.core)
        up = here.device(here.x, here.y, (here.z + 1) % 8, here.core)
        down = here.device(here.x, here.y, (here.z + 7) % 8, here.core)
        mate = here.mate()
        hi = here.y // 2
        p = (here.z % 2) * q
        o = q - p

        def rows(piece, core):
            dx, flip, start, count = piece
            block = (1 - hi if flip else hi) * 4 + (here.x + dx) % 4
            return feats.at[pl.ds(pl.multiple_of(block * BLK + core * h + start, 16), count), :]

        def add(to, piece, got, source=None):
            i = len(self.out)
            dst = rows(piece, here.core)
            self.out.append(remote(dst if source is None else source, dst, send.at[i], recv.at[i], to))
            land = rows(got, 1 - here.core if to is mate else here.core)
            self.into.append(remote(land, land, send.at[i], recv.at[i], to))

        mine = own.at[pl.ds(pl.multiple_of(here.core * h + p, e), q), :]
        N, F = False, True
        add(right, (0, N, p, q), (3, N, p, q), mine)
        add(left, (0, N, p, q), (1, N, p, q), mine)
        add(across, (0, N, p, q), (0, F, p, q), mine)
        add(right, (3, N, p, e), (2, N, p, e))
        add(left, (1, N, p + e, e), (2, N, p + e, e))
        add(right, (0, F, p, q), (3, F, p, q))
        add(left, (0, F, p, q), (1, F, p, q))
        add(up, (3, N, p, q), (3, N, o, q))
        add(down, (1, N, p, q), (1, N, o, q))
        add(up, (0, F, p, q), (0, F, o, q))
        for piece in ((3, N, p, q), (1, N, p, q), (0, F, p, q)):
            add(mate, piece, piece)
        add(across, (2, N, p + 32, 96), (2, F, p + 32, 96))
        add(down, (2, N, p, q), (2, N, o, q))
        add(up, (3, F, p, q), (3, F, o, q))
        add(down, (1, F, p, q), (1, F, o, q))
        for piece in ((2, N, p, q), (3, F, p, q), (1, F, p, q)):
            add(mate, piece, piece)
        add(up, (2, F, p, e), (2, F, o, e))
        add(down, (2, F, p + e, e), (2, F, o + e, e))
        add(mate, (2, F, p, q), (2, F, p, q))
        for piece in ((3, N, o, q), (1, N, o, q), (0, F, o, q)):
            add(mate, piece, piece)
        for piece in ((2, N, o, q), (3, F, o, q), (1, F, o, q), (2, F, o, q)):
            add(mate, piece, piece)
        add(right, (3, F, p, 16), (2, F, p, 16))
        add(left, (1, F, p + 16, 16), (2, F, p + 16, 16))

    def run(self, *steps):
        for got, go in steps:
            for i in got:
                self.into[i].wait_recv()
            for i in go:
                self.out[i].start()

    def first(self):
        self.run(((), (0, 1, 2)))

    def second(self):
        self.run(((0,), (3,)), ((1,), (4,)), ((2,), (5, 6, 9, 7, 8)), ((), (10, 11, 12)))

    def third(self):
        self.run(((3, 4), (13, 14, 17)))

    def third_across(self):
        self.run(((5,), (30, 15)), ((6,), (31, 16)), ((), (18, 19)), ((7,), (23,)), ((8,), (24,)), ((9,), (25,)))

    def fourth(self):
        self.run(((13, 30, 31), (20, 21, 22)))

    def fifth(self):
        self.run(((14,), (26,)), ((15,), (27,)), ((16,), (28,)), ((20, 21), (29,)))

    def sixth(self):
        self.run(((10, 11, 12, 17, 18, 19, *range(22, 30)), ()))

    def finish(self):
        for c in self.out:
            c.wait_send()


class Sum:
    def __init__(self, here, bufs, sems):
        self.here = here
        self.g, self.rc, self.hs, self.ra, self.ms, self.rb, self.out = bufs
        c_s, c_r, a_s, a_r, b_s, b_r, e_s, e_r, f_s, f_r = sems
        g, rc, hs, ra, ms, rb, out = bufs
        half = rc.shape[0]
        per = half // 16
        mate, me = here.mate(), here.member
        plane = list(here.plane())
        column = list(here.column(range(1, 8)))
        self.mine, self.other = here.core * half, (1 - here.core) * half
        self.half, self.per = half, per
        self.swap = remote(g.at[pl.ds(self.other, half)], rc, c_s, c_r, mate)
        self.to_plane = [
            remote(hs.at[pl.ds(q * per, per)], ra.at[me], a_s.at[q], a_r.at[me], d) for q, d in plane
        ]
        self.of_plane = [
            remote(hs.at[pl.ds(q * per, per)], ra.at[q], a_s.at[q], a_r.at[q], d) for q, d in plane
        ]

        self.to_column = [remote(ms, rb.at[here.z], b_s.at[z], b_r.at[here.z], d) for z, d in column]
        self.of_column = [remote(ms, rb.at[z], b_s.at[z], b_r.at[z], d) for z, d in column]
        self.slot = slot = pl.ds(self.mine + me * per, per)
        self.home_to, self.home_of, self.pass_to, self.pass_of = [], [], [], []
        for q, d in plane:
            at = out.at[pl.ds(self.mine + q * per, per)]
            self.home_to.append(remote(out.at[slot], out.at[slot], e_s.at[q], e_r.at[me], d))
            self.home_of.append(remote(at, at, e_s.at[q], e_r.at[q], d))
            self.pass_to.append(remote(at, at, f_s.at[q], f_r.at[q], mate))
        self.own_to = remote(out.at[slot], out.at[slot], f_s.at[me], f_r.at[me], mate)
        for q in range(16):
            at = out.at[pl.ds(self.other + q * per, per)]
            self.pass_of.append(remote(at, at, f_s.at[q], f_r.at[q], mate))

    def to_pair(self):
        self.swap.start()

    def to_the_plane(self):
        f32 = jnp.float32
        self.swap.wait_recv()
        both = self.g[pl.ds(self.mine, self.half)].astype(f32) + self.rc[...].astype(f32)
        self.hs[...] = both.astype(jnp.bfloat16)
        for c in self.to_plane:
            c.start()
        self.ra[self.here.member] = self.hs[pl.ds(self.here.member * self.per, self.per)]

    def to_the_column(self):
        for c in self.of_plane:
            c.wait_recv()
        self.ms[...] = jnp.sum(self.ra[...].astype(jnp.float32), axis=0).astype(jnp.bfloat16)
        for c in self.to_column:
            c.start()
        self.rb[self.here.z] = self.ms[...]

    def back_in_plane(self):
        for c in self.of_column:
            c.wait_recv()
        self.out[self.slot] = jnp.sum(self.rb[...].astype(jnp.float32), axis=0).astype(jnp.bfloat16)
        for c in self.home_to:
            c.start()
        self.own_to.start()

    def back_to_pair(self):
        for c, then in zip(self.home_of, self.pass_to):
            c.wait_recv()
            then.start()

    def received(self):
        for c in self.pass_of:
            c.wait_recv()

    def finish(self):
        sent = [self.swap, *self.to_plane, *self.to_column, *self.home_to, *self.pass_to]
        for c in [*sent, self.own_to]:
            c.wait_send()


def whole_kernel(
    fanout, cnt_ref, og_hbm, pa_hbm, l2_hbm, hs_hbm, ci_hbm, hf_hbm, cf_hbm, one_ref, two_ref,
    og, pa, l2, hs, ci, hu, cu, feats, rg, hp, c0, c1, acc, sems, tile_sems, g_send, g_recv, one_bufs, one_sems, two_bufs, two_sems,
):
    rows, dh = og.shape
    din = feats.shape[1]
    tile = 512
    hot_n = hf_hbm.shape[0] * 8
    here = Place()
    gather = Gather(here, hf_hbm, feats, g_send, g_recv)
    sums_one = [Sum(here, b, m) for b, m in zip(one_bufs, one_sems)]
    sum_two = Sum(here, two_bufs, two_sems)
    home = pl.ds(pl.multiple_of(lax.axis_index("clique") * BLK, BLK), BLK)
    pairs = [
        (l2_hbm, l2),
        (ci_hbm, ci),
        (hs_hbm, hs),
        (cf_hbm, feats.at[pl.ds(hot_n, cf_hbm.shape[0]), :]),
        (hf_hbm, feats.at[home, :]),
    ]
    copies = [pltpu.make_async_copy(s, d, sems.at[i]) for i, (s, d) in enumerate(pairs)]
    tiles = []
    for i in range(rows // tile):
        at = pl.ds(i * tile, tile)
        for n, (s, d) in enumerate(((og_hbm, og), (pa_hbm, pa))):
            tiles.append(pltpu.make_async_copy(s.at[at, :], d.at[at, :], tile_sems.at[2 * i + n]))
    barrier = pltpu.get_barrier_semaphore()
    peers = [here.mate()] + [d for _, d in here.plane()] + [d for _, d in here.column(range(1, 8))]
    for d in peers:
        pl.semaphore_signal(barrier, inc=1, device_id=d, device_id_type=MESH)
    for c in [copies[1], copies[0], *tiles, *copies[2:]]:
        c.start()
    pl.semaphore_wait(barrier, len(peers))
    gather.first()
    count = cnt_ref[0]
    acc[:dh, :] = jnp.zeros((dh, dh), jnp.float32)
    copies[1].wait()
    split_indices(ci, cu)
    copies[0].wait()
    for i in range(rows // tile):
        tiles[2 * i].wait()
        tiles[2 * i + 1].wait()
        at = slice(i * tile, i * tile + tile)
        live = (lax.broadcasted_iota(jnp.int32, (tile, 1), 0) + i * tile) < count
        o = og[at, :]
        masked = jnp.where(live, o, jnp.zeros_like(o))
        p = pa[at, :]
        back = lax.dot_general(
            masked, l2[...], (((1,), (1,)), ((), ())), preferred_element_type=jnp.float32
        )
        rg[at, :] = jnp.where(p > 0, back, 0.0).astype(jnp.bfloat16)
        activ = jnp.maximum(p, jnp.zeros_like(p))
        acc[:dh, :] += lax.dot_general(
            activ, masked, (((0,), (0,)), ((), ())), preferred_element_type=jnp.float32
        )
        build_counts(ci, cu, 0, c0, (i, rows // tile))
    sum_two.g[...] = acc[:dh, :].reshape(dh // 8, 8, dh).astype(jnp.bfloat16)
    sum_two.to_pair()
    copies[2].wait()
    split_indices(hs, hu)
    n_hot = hot_n // BLK

    def step(refs, block, c_new, c_old, base):
        if refs is not None:
            build_counts(*refs, block, c_new)
        p = jnp.dot(c_old[...], rg[...], preferred_element_type=jnp.float32)
        size = BLK // 8
        for b in range(8):
            at = pl.ds(pl.multiple_of(base + b * size, size), size)
            scaled = p[b * size : b * size + size] * (field_scale(b) / fanout)
            hp[at, :] = scaled.astype(jnp.bfloat16)

    cold, warm = (ci, cu), (hs, hu)
    step(cold, 1, c1, c0, hot_n)
    gather.second()
    step(cold, 2, c0, c1, hot_n + BLK)
    step(cold, 3, c1, c0, hot_n + 2 * BLK)
    step(warm, 0, c0, c1, hot_n + 3 * BLK)

    def hot(i, carry):
        step(warm, 2 * i + 1, c1, c0, 2 * i * BLK)
        step(warm, 2 * i + 2, c0, c1, (2 * i + 1) * BLK)

        @pl.when(i == 0)
        def _():
            gather.third()

        @pl.when(i == 1)
        def _():
            gather.third_across()

        return carry

    lax.fori_loop(0, n_hot // 2 - 1, hot, 0)
    gather.fourth()
    step(warm, n_hot - 1, c1, c0, (n_hot - 2) * BLK)
    sum_two.to_the_plane()
    step(None, 0, c0, c1, (n_hot - 1) * BLK)
    for c in copies[3:]:
        c.wait()
    turned = (((0,), (0,)), ((), ()))
    acc[...] = lax.dot_general(
        feats[hot_n:, :], hp[hot_n:, :], turned, preferred_element_type=jnp.float32
    )
    gather.fifth()
    gather.sixth()
    sum_two.to_the_column()
    width = din // len(sums_one)

    def some_sums(n):
        at = slice(n * width, n * width + width)
        sums = acc[at, :] + lax.dot_general(
            feats[:hot_n, at], hp[:hot_n, :], turned, preferred_element_type=jnp.float32
        )
        sums_one[n].g[...] = sums.reshape(width // 8, 8, dh).astype(jnp.bfloat16)
        sums_one[n].to_pair()

    some_sums(0)
    some_sums(1)
    sums_one[0].to_the_plane()
    some_sums(2)
    sums_one[1].to_the_plane()
    sums_one[2].to_the_plane()
    sum_two.back_in_plane()
    for one in sums_one:
        one.to_the_column()
    for one in sums_one:
        one.back_in_plane()
    sum_two.back_to_pair()
    for one in sums_one:
        one.back_to_pair()
    sum_two.received()
    two_ref[...] = sum_two.out[...]
    for n, one in enumerate(sums_one):
        one.received()
        one_ref[n * width // 8 : (n + 1) * width // 8] = one.out[...]
    gather.finish()
    sum_two.finish()
    for one in sums_one:
        one.finish()


def sum_scratch(rows, dh):
    vm, dma, bf16 = pltpu.VMEM, pltpu.SemaphoreType.DMA, jnp.bfloat16
    units = rows // 8
    half, per = units // 2, units // 32
    bufs = (
        vm((units, 8, dh), bf16),
        vm((half, 8, dh), bf16),
        vm((half, 8, dh), bf16),
        vm((16, per, 8, dh), bf16),
        vm((per, 8, dh), bf16),
        vm((8, per, 8, dh), bf16),
        vm((units, 8, dh), bf16),
    )
    sems = [dma, dma] + [dma((n,)) for n in (16, 16, 8, 8, 16, 16, 16, 16)]
    return bufs, tuple(sems)


def whole_call(fanout, og, pa, cnt, l2, hs, ci, hf, cf):
    vm, dma = pltpu.VMEM, pltpu.SemaphoreType.DMA
    hbm = pl.BlockSpec(memory_space=pltpu.HBM)
    bf16 = jnp.bfloat16
    rows, dh = og.shape
    din = hf.shape[1]
    slots = hf.shape[0] * 8 + cf.shape[0]
    chunks = [sum_scratch(din // 3, dh) for _ in range(3)]
    one_bufs, one_sems = tuple(c[0] for c in chunks), tuple(c[1] for c in chunks)
    two_bufs, two_sems = sum_scratch(dh, dh)
    return pl.pallas_call(
        functools.partial(whole_kernel, fanout),
        out_shape=(
            jax.ShapeDtypeStruct((din // 8, 8, dh), bf16),
            jax.ShapeDtypeStruct((dh // 8, 8, dh), bf16),
        ),
        in_specs=[pl.BlockSpec(memory_space=pltpu.SMEM)] + [hbm] * 7,
        out_specs=[pl.BlockSpec(memory_space=vm)] * 2,
        scratch_shapes=[
            vm((rows, dh), bf16),
            vm((rows, dh), bf16),
            vm((dh, dh), bf16),
            vm((hs.shape[1], rows), jnp.int32),
            vm((ci.shape[1], rows), jnp.int32),
            vm((hs.shape[1], rows), jnp.int32),
            vm((ci.shape[1], rows), jnp.int32),
            vm((slots, din), bf16),
            vm((rows, dh), bf16),
            vm((slots, dh), bf16),
            vm((BLK, rows), bf16),
            vm((BLK, rows), bf16),
            vm((din, dh), jnp.float32),
            dma((5,)),
            dma((2 * (rows // 512),)),
            dma((32,)),
            dma((32,)),
            one_bufs,
            one_sems,
            two_bufs,
            two_sems,
        ],
        compiler_params=pltpu.CompilerParams(
            collective_id=0, has_side_effects=True, vmem_limit_bytes=58 << 20
        ),
    )(cnt, og, pa, l2, hs.T, ci.T, hf, cf)


def on_device(
    out_grad, pre_act, batch_count, layer_two, hot_slots, cold_index, hot_feats, cold_feats
):
    fanout = hot_slots.shape[1] + cold_index.shape[1]
    one, two = whole_call(
        fanout, out_grad, pre_act, batch_count, layer_two, hot_slots, cold_index, hot_feats, cold_feats
    )
    dh = out_grad.shape[1]
    return one.reshape(-1, dh).astype(jnp.float32), two.reshape(-1, dh).astype(jnp.float32)


def solution(mesh):
    placed = (
        P(("clique", "copy"), None),
        P(("clique", "copy"), None),
        P(("clique", "copy")),
        P(),
        P(("clique", "copy"), None),
        P(("clique", "copy"), None),
        P("clique", None),
        P(("clique", "copy"), None),
    )
    return jax.shard_map(
        on_device, mesh=mesh, in_specs=placed, out_specs=(P(), P()), check_vma=False
    )
```
